128 devices in a mesh: slab: 16 (over x, z_hi, core), xy: 8 (over z_lo, y).
Axes of the slice: x: 4, y: 4, z: 4 (z_hi: 2, z_lo: 2; z = z_hi * 2 + z_lo), core: 2. Of those that a mesh axis runs over, the one named last changes fastest.
Arguments:
- volume: float32 [32, 64, 512], P('slab', 'xy'), may hold values from 0 to 1
- footprint: bfloat16 [32, 64, 4, 2, 128, 256], P('slab', 'xy'), may hold values from 0.049804688 to 1
- tile_block: int32 [32, 64, 4, 2], P('slab', 'xy'), may hold values from 0 to 511, as said below
- tile_cells: int32 [32, 64, 4, 2], P('slab', 'xy'), may hold values from 1 to 256, as said below
- measured: float32 [2, 131072], replicated, may hold values from 0 to 512
Outputs:
- updated: float32 [32, 64, 512], P('slab', 'xy')
- correction: float32 [2, 131072], P(None, ('slab', 'xy'))
The draws below stay inside these ranges and needn't reach their ends.
Inputs may be any that keep to these rules, and one draw needn't show every extreme that they name: `tile_cells`: at least one tile of some view has all 256 cells live. `tile_block`: A tile's block lies in detector row about plane * 2, off by at most one below and 2 above (within the detector); its column block follows the tile's place along the row for even views and the row's place in the plane for odd views, off by at most one.
All inputs are finite; a program needn't handle non-finite values.
Results may differ from the reference program's by a relative error of at most 0.0003.
Values may be sent and summed in bfloat16 or wider, within the bound.
A program may use at most 64 MiB of HBM per device.

```python
import jax
import jax.numpy as jnp
from jax import lax

PLANES = 32
NX = 64
NY = 512
TV = 128
NYB = 4
VIEWS = 2
DROWS = 64
DCOLS = 2048
DET = 131072
TD = 256
NB = 512


def draw_tile_cells(key, part):
    shape = (PLANES, NX, NYB, VIEWS)
    first, second = jax.random.split(jax.random.fold_in(key, 11))
    cells = jax.random.randint(first, shape, 1, TD + 1).reshape(-1)
    spot = jax.random.randint(second, (), 0, cells.shape[0])
    cells = jnp.where(jnp.arange(cells.shape[0]) == spot, TD, cells)
    return cells.reshape(shape).astype(jnp.int32)


def draw_tile_block(key, part):
    shape = (PLANES, NX, NYB, VIEWS)
    key_row, key_col = jax.random.split(jax.random.fold_in(key, 23))
    per_row = DCOLS // TD
    lift = max(DROWS // PLANES, 1)
    plane = jnp.arange(PLANES, dtype=jnp.int32)[:, None, None, None]
    xrow = jnp.arange(NX, dtype=jnp.int32)[None, :, None, None]
    tile = jnp.arange(NYB, dtype=jnp.int32)[None, None, :, None]
    view = jnp.arange(VIEWS, dtype=jnp.int32)[None, None, None, :]
    det_row = plane * DROWS // PLANES + jax.random.randint(key_row, shape, -1, lift + 1)
    det_row = jnp.clip(det_row, 0, DROWS - 1)
    along = jnp.where(view % 2 == 0, tile * per_row // NYB, xrow * per_row // NX)
    det_col = jnp.clip(along + jax.random.randint(key_col, shape, -1, 2), 0, per_row - 1)
    return (det_row * per_row + det_col).astype(jnp.int32)


def levels(rng, dims, pieces, smallest, top_value):
    def one(position, blocks):
        steps = jax.random.uniform(jax.random.fold_in(jax.random.fold_in(rng, 6), position), (blocks,), jnp.float32, smallest / len(pieces), top_value / len(pieces))
        return jnp.repeat(jnp.exp(steps), dims[position] // blocks).reshape((-1,) + (1,) * (len(dims) - position - 1))

    gain = one(*pieces[0])
    for cut in pieces[1:]:
        gain = gain * one(*cut)
    return gain


def setup_inputs(seed: int = 0) -> dict:
    key_list = jax.random.split(jax.random.key(seed), 6)
    volume = jnp.clip(1.0 * jax.random.uniform(key_list[0], (PLANES, NX, NY), jnp.float32) ** levels(key_list[0], (PLANES, NX, NY), ((0, 16), (1, 8)), -0.2, 0.2), 0.0, 1.0)
    footprint = jnp.clip(0.049804688 + 0.9501953 * jax.random.uniform(key_list[1], (PLANES, NX, NYB, VIEWS, TV, TD), jnp.float32) ** levels(key_list[1], (PLANES, NX, NYB, VIEWS, TV, TD), ((0, 16), (1, 8)), -0.2, 0.2), 0.049804688, 1.0).astype(jnp.bfloat16)
    tile_block = draw_tile_block(jax.random.fold_in(key_list[5], 71), 0)
    tile_cells = draw_tile_cells(jax.random.fold_in(key_list[5], 71), 0)
    measured = jnp.clip(jax.random.uniform(key_list[4], (VIEWS, DET), jnp.float32, 0.0, 512.0), 0.0, 512.0)
    return dict(volume=volume, footprint=footprint, tile_block=tile_block, tile_cells=tile_cells, measured=measured)


RELAX = 1.0
TV_RATE = 0.8
SMOOTHING = 0.01

def masked_plane(foot_plane, cells_plane):
    lane = jnp.arange(TD, dtype=jnp.int32)
    live = lane[None, None, None, :] < cells_plane[:, :, :, None]
    return jnp.where(live[:, :, :, None, :], foot_plane, jnp.zeros((), jnp.bfloat16))

def tv_slope(padded):
    base = padded[:-1, :-1, :-1]
    diff_a = padded[1:, :-1, :-1] - base
    diff_b = padded[:-1, 1:, :-1] - base
    diff_e = padded[:-1, :-1, 1:] - base
    size = jnp.sqrt(diff_a * diff_a + diff_b * diff_b + diff_e * diff_e + SMOOTHING)
    unit_a = diff_a / size
    unit_b = diff_b / size
    unit_e = diff_e / size
    total = unit_a + unit_b + unit_e
    return -total[1:, 1:, 1:] + unit_a[:-1, 1:, 1:] + unit_b[1:, :-1, 1:] + unit_e[1:, 1:, :-1]

def reference(volume, footprint, tile_block, tile_cells, measured):
    blocks = jnp.arange(NB, dtype=jnp.int32)

    def forward(carry, inputs):
        vol_plane, foot_plane, block_plane, cells_plane = inputs
        weights = masked_plane(foot_plane, cells_plane).astype(jnp.float32)
        voxels = vol_plane.astype(jnp.bfloat16).astype(jnp.float32).reshape(NX, NYB, TV)
        contrib = jnp.einsum('abj,abvjc->abvc', voxels, weights)
        rays = lax.optimization_barrier(jnp.sum(weights, axis=3))
        onehot = (block_plane[:, :, :, None] == blocks).astype(jnp.float32)
        proj = jnp.einsum('abvn,abvc->vnc', onehot, contrib, precision=lax.Precision.HIGHEST)
        ray = jnp.einsum('abvn,abvc->vnc', onehot, rays, precision=lax.Precision.HIGHEST)
        return ((carry[0] + proj, carry[1] + ray), None)
    start = jnp.zeros((VIEWS, NB, TD), jnp.float32)
    (projected, ray_weight), _ = lax.scan(forward, (start, start), (volume, footprint, tile_block, tile_cells))
    projected = projected.reshape(VIEWS, DET)
    ray_weight = ray_weight.reshape(VIEWS, DET)
    correction = (measured - projected) / jnp.maximum(ray_weight, 1.0)
    correction_b = correction.astype(jnp.bfloat16).reshape(VIEWS, NB, TD)
    view_ids = jnp.arange(VIEWS, dtype=jnp.int32)

    def backward(inputs):
        foot_plane, block_plane, cells_plane = inputs
        weights = masked_plane(foot_plane, cells_plane).astype(jnp.float32)
        picked = correction_b[view_ids[None, None, :], block_plane].astype(jnp.float32)
        back = jnp.einsum('abvjc,abvc->abj', weights, picked)
        column = lax.optimization_barrier(jnp.sum(weights, axis=(2, 4)))
        return (back / column).reshape(NX, NY)
    shift = lax.map(backward, (footprint, tile_block, tile_cells))
    sart = jnp.maximum(volume + RELAX * shift, 0.0)
    step_gap = sart - volume
    update_norm = jnp.sqrt(jnp.sum(step_gap * step_gap))
    current = sart
    for turn in range(2):
        slope = tv_slope(jnp.pad(current, 1))
        scale = jnp.sqrt(jnp.sum(slope * slope) + 1e-06)
        current = current - TV_RATE * update_norm / scale * slope
    return (current, correction)
```

```python
import functools

import jax
import jax.numpy as jnp
from jax import lax
from jax.experimental import pallas as pl
from jax.experimental.pallas import tpu as pltpu
from jax.sharding import PartitionSpec as P

TV_RATE = 0.8
SMOOTHING = 0.01
MESH = pl.DeviceIdType.MESH
F32 = jnp.float32
BF16 = jnp.bfloat16
GROUPS = 12


def iota(shape, dim):
    return lax.broadcasted_iota(jnp.int32, shape, dim)


def lane_next(x):
    return jnp.where(iota(x.shape, 2) < x.shape[2] - 1, pltpu.roll(x, x.shape[2] - 1, 2), 0.0)


def units(field):
    base = field[:-1]
    diff_a = field[1:] - base
    diff_b = pltpu.roll(base, base.shape[1] - 1, 1) - base
    diff_e = lane_next(base) - base
    inv = lax.rsqrt(diff_a * diff_a + diff_b * diff_b + diff_e * diff_e + SMOOTHING)
    return diff_a * inv, diff_b * inv, diff_e * inv


def tv_slope(field):
    unit_a, unit_b, unit_e = units(field)
    core = field[1:-1]
    prev_b = pltpu.roll(unit_b[1:], 1, 1)
    edge = core * lax.rsqrt(core * core + SMOOTHING)
    prev_e = jnp.where(iota(core.shape, 2) == 0, edge, pltpu.roll(unit_e[1:], 1, 2))
    return unit_a[:-1] + prev_b + prev_e - (unit_a + unit_b + unit_e)[1:]


def lane_partial(x):
    rows = jnp.sum(x, axis=0)
    parts = rows[:, :128]
    for c in range(1, x.shape[2] // 128):
        parts = parts + rows[:, c * 128 : (c + 1) * 128]
    return jnp.sum(parts, axis=0, keepdims=True)


def kernel(
    ns, nx,
    vol_hbm, foot_hbm, blk_hbm, cells_hbm, meas_hbm,
    upd_ref, cor_ref,
    vol, wbuf, blk, cells, meas, bcol, ccol, onehot, contrib,
    send_a, recv_a, total, send_b, recv_b, lhs_b, num, den,
    ublk, rows_lo, rows_hi, uside, hnext, hprev,
    red_s, red_xy, red_slab,
    sem_w, sem_in, sem_s, sem_a, sem_b, sem_c, sem_cs, sem_r,
):
    s = lax.axis_index("slab")
    r = lax.axis_index("xy")
    groups = wbuf.shape[0]

    ins = [
        pltpu.make_async_copy(blk_hbm, blk, sem_in.at[0]),
        pltpu.make_async_copy(cells_hbm, cells, sem_in.at[1]),
        pltpu.make_async_copy(vol_hbm, vol, sem_in.at[2]),
        pltpu.make_async_copy(
            meas_hbm.at[:, pl.ds(pl.multiple_of((s * nx + r) * 1024, 1024), 1024)], meas, sem_in.at[3]
        ),
    ]
    for c in ins:
        c.start()

    def load(i):
        return pltpu.make_async_copy(foot_hbm.at[i], wbuf.at[i], sem_w.at[i])

    @pl.loop(0, groups)
    def _(i):
        load(i).start()

    barrier = pltpu.get_barrier_semaphore()

    def hello(ds, dr):
        pl.semaphore_signal(barrier, inc=1, device_id=(ds, dr), device_id_type=MESH)

    @pl.loop(1, nx)
    def _(d):
        rp = lax.rem(r + d, nx)
        hello(s, rp)

        @pl.when(s > 0)
        def _():
            hello(s - 1, rp)

        @pl.when(s < ns - 1)
        def _():
            hello(s + 1, rp)

    @pl.loop(1, ns)
    def _(d):
        hello(lax.rem(s + d, ns), r)

    recv_b[GROUPS:] = jnp.zeros((16 - GROUPS,) + recv_b.shape[1:], BF16)

    @pl.when(s == 0)
    def _():
        recv_b[0:2] = jnp.zeros((2,) + recv_b.shape[1:], BF16)
        uside[0] = jnp.zeros(uside.shape[1:], F32)
        hnext[0] = jnp.zeros(hnext.shape[1:], F32)
        hprev[0] = jnp.zeros(hprev.shape[1:], F32)

    @pl.when(s == ns - 1)
    def _():
        recv_b[10:12] = jnp.zeros((2,) + recv_b.shape[1:], BF16)
        uside[1] = jnp.zeros(uside.shape[1:], F32)
        hnext[2] = jnp.zeros(hnext.shape[1:], F32)
        hprev[2] = jnp.zeros(hprev.shape[1:], F32)

    @pl.when(r == 0)
    def _():
        hprev[...] = jnp.zeros(hprev.shape, F32)

    @pl.when(r == nx - 1)
    def _():
        hnext[...] = jnp.zeros(hnext.shape, F32)

    ins[0].wait()
    ins[1].wait()
    for p in range(2):
        for t in range(4):
            bcol[p, 2 * t : 2 * t + 2, 0:8] = blk[p, t]
            ccol[p, 2 * t : 2 * t + 2, 0:8] = cells[p, t]
    lane = iota((8, 128), 1)
    view4 = (iota((8, 128), 0) & 1) * 4
    first = (4 * s - 1) * 8
    for p in range(2):
        blk_p = bcol[p]
        cells_p = ccol[p]
        for x in range(8):
            i = p * 8 + x
            near = jnp.broadcast_to(blk_p[:, x : x + 1], (8, 128)) - first
            target = (near >> 2) * 8 + view4 + (near & 3)
            onehot[i * 8 : i * 8 + 8, :] = jnp.where(lane == target, 1.0, 0.0)
            den[i * 8 : i * 8 + 8, :] = jnp.broadcast_to(cells_p[:, x : x + 1], (8, 128))
    ins[2].wait()

    row16 = iota((16, 128), 0)

    @pl.loop(0, groups)
    def _(i):
        vox = vol[pl.ds(i, 1), :]
        parts = []
        for k in range(8):
            t = k // 2
            spread = jnp.broadcast_to(vox[:, t * 128 : (t + 1) * 128], (16, 128))
            parts.append(
                jnp.where(row16 == k, spread, jnp.where(row16 == k + 8, 1.0, 0.0)).astype(BF16)
            )
        left = jnp.concatenate(parts, axis=1)
        load(i).wait()
        out = jnp.dot(left, wbuf[i], preferred_element_type=F32)
        at = pl.ds(pl.multiple_of(i * 8, 8), 8)
        limit = den[at, :]
        limit = jnp.concatenate([limit, limit], axis=1)
        live = iota((8, 256), 1) < limit
        contrib[at, 0:256] = jnp.where(live, out[0:8], 0.0)
        contrib[at, 256:512] = jnp.where(live, out[8:16], 0.0)

    hot = onehot[...].astype(BF16)
    hot_t = jnp.transpose(onehot[...]).astype(BF16)
    whole = contrib[...]
    high = whole.astype(BF16)
    low = (whole - high.astype(F32)).astype(BF16)
    sums = jnp.dot(hot_t, high, preferred_element_type=F32) + jnp.dot(
        hot_t, low, preferred_element_type=F32
    )
    send_a[...] = sums.reshape(16, 8, 512)

    count = 7 + (ns - 1) + jnp.where(s > 0, nx - 1, 0) + jnp.where(s < ns - 1, nx - 1, 0)
    pl.semaphore_wait(barrier, count)

    def remote(src, dst, sem_send, sem_recv, ds, dr):
        return pltpu.make_async_remote_copy(
            src_ref=src, dst_ref=dst, send_sem=sem_send, recv_sem=sem_recv,
            device_id=(ds, dr), device_id_type=MESH,
        )

    @pl.when(s > 0)
    def _():
        for g in range(2):
            remote(send_a.at[g], recv_a.at[nx - 1 + r], sem_s.at[1], sem_a.at[1], s - 1, nx - 2 + g).start()

    @pl.when(s < ns - 1)
    def _():
        for g in range(2):
            remote(send_a.at[10 + g], recv_a.at[nx - 1 + r], sem_s.at[2], sem_a.at[1], s + 1, g).start()

    @pl.loop(1, nx)
    def _(d):
        rp = lax.rem(r + d, nx)
        remote(send_a.at[2 + rp], recv_a.at[d - 1], sem_s.at[0], sem_a.at[0], s, rp).start()

    ins[3].wait()
    m = meas[...]
    seen = jnp.concatenate(
        [m[v : v + 1, q * 256 : (q + 1) * 256] for v in range(2) for q in range(4)], axis=0
    )
    own = send_a[2 + r]
    remote(send_a.at[pl.ds(0, nx - 1)], recv_a.at[pl.ds(0, nx - 1)], sem_s.at[0], sem_a.at[0], s, r).wait_recv()
    total[...] = own + jnp.sum(recv_a[0 : nx - 1], axis=0)
    low_edge = jnp.logical_and(r < 2, s > 0)
    high_edge = jnp.logical_and(r >= nx - 2, s < ns - 1)

    @pl.when(jnp.logical_or(low_edge, high_edge))
    def _():
        remote(send_a.at[pl.ds(0, nx)], recv_a.at[pl.ds(nx - 1, nx)], sem_s.at[0], sem_a.at[1], s, r).wait_recv()
        total[...] += jnp.sum(recv_a[nx - 1 : 2 * nx - 1], axis=0)

    tot = total[...]
    corr = (seen - tot[:, 0:256]) / jnp.maximum(tot[:, 256:512], 1.0)
    send_b[...] = corr.astype(BF16)
    recv_b[2 + r] = corr.astype(BF16)

    @pl.when(low_edge)
    def _():
        @pl.loop(0, nx)
        def _(rp):
            remote(send_b, recv_b.at[10 + r], sem_s.at[4], sem_b.at[2], s - 1, rp).start()

    @pl.when(high_edge)
    def _():
        @pl.loop(0, nx)
        def _(rp):
            remote(send_b, recv_b.at[r - (nx - 2)], sem_s.at[4], sem_b.at[1], s + 1, rp).start()

    @pl.loop(1, nx)
    def _(d):
        rp = lax.rem(r + d, nx)
        remote(send_b, recv_b.at[2 + r], sem_s.at[3], sem_b.at[0], s, rp).start()

    for v in range(2):
        for q in range(4):
            cor_ref[v : v + 1, q * 256 : (q + 1) * 256] = corr[v * 4 + q : v * 4 + q + 1, :]

    limit = den[...]
    limit = jnp.concatenate([limit, limit], axis=1)
    live = iota((128, 256), 1) < limit
    live3 = jnp.where(live, 1.0, 0.0).reshape(16, 8, 256)

    remote(recv_b.at[pl.ds(0, nx - 1)], recv_b.at[pl.ds(0, nx - 1)], sem_s.at[3], sem_b.at[0], s, r).wait_recv()

    @pl.when(s > 0)
    def _():
        remote(recv_b.at[pl.ds(0, 2)], recv_b.at[pl.ds(0, 2)], sem_s.at[3], sem_b.at[1], s, r).wait_recv()

    @pl.when(s < ns - 1)
    def _():
        remote(recv_b.at[pl.ds(10, 2)], recv_b.at[pl.ds(10, 2)], sem_s.at[3], sem_b.at[2], s, r).wait_recv()

    table = recv_b[...].astype(F32).reshape(128, 256).astype(BF16)
    picked = jnp.dot(hot, table, preferred_element_type=F32)
    picked = jnp.where(live, picked, 0.0).reshape(16, 8, 256)
    lhs_b[...] = jnp.concatenate([picked, live3], axis=1).astype(BF16)

    row8 = iota((8, 128), 0)

    @pl.loop(0, 2)
    def _(p):
        tops, bottoms = [], []
        for x in range(8):
            i = p * 8 + x
            out = lax.dot_general(
                lhs_b[i], wbuf[i], (((1,), (1,)), ((), ())), preferred_element_type=F32
            )
            for rows, into in ((out[0:8], tops), (out[8:16], bottoms)):
                lanes = []
                for t in range(4):
                    k = 2 * t
                    both = jnp.where(row8 == k, rows[:, k * 128 : k * 128 + 128], 0.0) + jnp.where(
                        row8 == k + 1, rows[:, k * 128 + 128 : k * 128 + 256], 0.0
                    )
                    lanes.append(jnp.sum(both, axis=0, keepdims=True))
                into.append(jnp.concatenate(lanes, axis=1))
        num[pl.ds(pl.multiple_of(p * 8, 8), 8), :] = jnp.concatenate(tops, axis=0)
        num[pl.ds(pl.multiple_of(p * 8 + 16, 8), 8), :] = jnp.concatenate(bottoms, axis=0)

    before = vol[...]
    sart = jnp.maximum(before + num[0:groups] / num[groups : 2 * groups], 0.0)
    gap = (sart - before).reshape(2, 8, 512)
    cells3 = sart.reshape(2, 8, 512)

    ublk[...] = cells3
    rows_lo[...] = cells3[:, 0:2, :]
    rows_hi[...] = cells3[:, 6:8, :]

    def exists(ds, dr):
        ok = None
        for cond in (
            [s > 0] if ds < 0 else [s < ns - 1] if ds > 0 else []
        ) + ([r > 0] if dr < 0 else [r < nx - 1] if dr > 0 else []):
            ok = cond if ok is None else jnp.logical_and(ok, cond)
        return ok

    def halo(n, ds, dr):
        if dr == 0:
            src, dst = ublk, uside.at[1 if ds < 0 else 0]
        elif dr < 0:
            src, dst = rows_lo, hnext.at[1 - ds]
        else:
            src, dst = rows_hi, hprev.at[1 - ds]
        return remote(src, dst, sem_cs.at[n], sem_c.at[n], s + ds, r + dr)

    offsets = [(ds, dr) for ds in (-1, 1) for dr in (-1, 1, 0)] + [(0, -1), (0, 1)]
    for n, (ds, dr) in enumerate(offsets):

        @pl.when(exists(ds, dr))
        def _():
            halo(n, ds, dr).start()

    for n, (ds, dr) in enumerate(offsets):

        @pl.when(exists(-ds, -dr))
        def _():
            halo(n, ds, dr).wait_recv()

    def padded(main, after, before):
        return jnp.concatenate([main, after, jnp.zeros((4, 512), F32), before], axis=0)[None]

    field = jnp.concatenate(
        [padded(uside[0, p], hnext[0, p], hprev[0, p]) for p in range(2)]
        + [padded(ublk[p], hnext[1, p], hprev[1, p]) for p in range(2)]
        + [padded(uside[1, p], hnext[2, p], hprev[2, p]) for p in range(2)],
        axis=0,
    )
    slope = tv_slope(field)

    def reduce_all(n, parts):
        red_s[2 * n] = parts

        @pl.loop(1, nx)
        def _(d):
            rp = lax.rem(r + d, nx)
            remote(red_s.at[2 * n], red_xy.at[n, d - 1], sem_s.at[5 + 2 * n], sem_r.at[2 * n], s, rp).start()

        remote(
            red_xy.at[n, pl.ds(0, nx - 1)], red_xy.at[n, pl.ds(0, nx - 1)],
            sem_s.at[5 + 2 * n], sem_r.at[2 * n], s, r,
        ).wait_recv()
        parts = parts + jnp.sum(red_xy[n, 0 : nx - 1], axis=0)
        red_s[2 * n + 1] = parts

        @pl.loop(1, ns)
        def _(d):
            sp = lax.rem(s + d, ns)
            remote(
                red_s.at[2 * n + 1], red_slab.at[n, d - 1], sem_s.at[6 + 2 * n], sem_r.at[2 * n + 1], sp, r
            ).start()

        remote(
            red_slab.at[n, pl.ds(0, ns - 1)], red_slab.at[n, pl.ds(0, ns - 1)],
            sem_s.at[6 + 2 * n], sem_r.at[2 * n + 1], s, r,
        ).wait_recv()
        return parts + jnp.sum(red_slab[n, 0 : ns - 1], axis=0)

    own_slope = slope[1:3, 0:8, :]
    both = reduce_all(0, jnp.concatenate([lane_partial(gap * gap), lane_partial(own_slope * own_slope)], axis=1))
    rate = TV_RATE * jnp.sqrt(jnp.sum(both[:, 0:128], axis=1, keepdims=True))
    scale = jnp.sqrt(jnp.sum(both[:, 128:256], axis=1, keepdims=True) + 1e-06)
    inner = field[1:5]
    plane = iota(inner.shape, 0) + jnp.where(s > 0, 1, 0)
    row = iota(inner.shape, 1)
    inside = jnp.logical_and(plane >= 1, iota(inner.shape, 0) < jnp.where(s < ns - 1, 4, 3))
    inside = jnp.logical_and(inside, row < jnp.where(r > 0, 16, 12))
    inside = jnp.logical_and(inside, jnp.logical_or(row < 8, jnp.logical_or(row >= 12, r < nx - 1)))
    step = (rate / scale).reshape(1, 1, 1)
    first_u = jnp.where(inside, inner - step * slope, 0.0)
    slope2 = tv_slope(first_u)[:, 0:8, :]
    part2 = lane_partial(slope2 * slope2)
    both2 = reduce_all(1, jnp.concatenate([part2, part2], axis=1))
    scale2 = jnp.sqrt(jnp.sum(both2[:, 0:128], axis=1, keepdims=True) + 1e-06)
    step2 = (rate / scale2).reshape(1, 1, 1)
    upd_ref[...] = first_u[1:3, 0:8, :] - step2 * slope2

    remote(send_a.at[pl.ds(0, nx - 1)], recv_a.at[pl.ds(0, nx - 1)], sem_s.at[0], sem_a.at[0], s, r).wait_send()
    remote(recv_b.at[pl.ds(0, nx - 1)], recv_b.at[pl.ds(0, nx - 1)], sem_s.at[3], sem_b.at[0], s, r).wait_send()

    @pl.when(s > 0)
    def _():
        remote(send_a.at[pl.ds(0, 2)], recv_a.at[pl.ds(0, 2)], sem_s.at[1], sem_a.at[0], s, r).wait_send()

    @pl.when(s < ns - 1)
    def _():
        remote(send_a.at[pl.ds(0, 2)], recv_a.at[pl.ds(0, 2)], sem_s.at[2], sem_a.at[0], s, r).wait_send()

    @pl.when(jnp.logical_or(low_edge, high_edge))
    def _():
        remote(recv_b.at[pl.ds(0, nx)], recv_b.at[pl.ds(0, nx)], sem_s.at[4], sem_b.at[0], s, r).wait_send()

    for n, (ds, dr) in enumerate(offsets):

        @pl.when(exists(ds, dr))
        def _():
            halo(n, ds, dr).wait_send()

    for n in range(2):
        remote(
            red_xy.at[n, pl.ds(0, nx - 1)], red_xy.at[n, pl.ds(0, nx - 1)],
            sem_s.at[5 + 2 * n], sem_r.at[0], s, r,
        ).wait_send()
        remote(
            red_slab.at[n, pl.ds(0, ns - 1)], red_slab.at[n, pl.ds(0, ns - 1)],
            sem_s.at[6 + 2 * n], sem_r.at[0], s, r,
        ).wait_send()


def body(ns, nx, volume, footprint, tile_block, tile_cells, measured):
    any_space = pl.BlockSpec(memory_space=pltpu.HBM)
    vmem = pl.BlockSpec(memory_space=pltpu.VMEM)
    dma = pltpu.SemaphoreType.DMA
    call = pl.pallas_call(
        functools.partial(kernel, ns, nx),
        out_shape=(
            jax.ShapeDtypeStruct((2, 8, 512), F32),
            jax.ShapeDtypeStruct((2, 1024), F32),
        ),
        in_specs=[any_space] * 5,
        out_specs=(vmem, vmem),
        scratch_shapes=[
            pltpu.VMEM((16, 512), F32),
            pltpu.VMEM((16, 1024, 256), BF16),
            pltpu.VMEM((2, 4, 2, 8), jnp.int32),
            pltpu.VMEM((2, 4, 2, 8), jnp.int32),
            pltpu.VMEM((2, 1024), F32),
            pltpu.VMEM((2, 8, 128), jnp.int32),
            pltpu.VMEM((2, 8, 128), jnp.int32),
            pltpu.VMEM((128, 128), F32),
            pltpu.VMEM((128, 512), F32),
            pltpu.VMEM((16, 8, 512), F32),
            pltpu.VMEM((2 * nx - 1, 8, 512), F32),
            pltpu.VMEM((8, 512), F32),
            pltpu.VMEM((8, 256), BF16),
            pltpu.VMEM((16, 8, 256), BF16),
            pltpu.VMEM((16, 16, 256), BF16),
            pltpu.VMEM((32, 512), F32),
            pltpu.VMEM((128, 128), jnp.int32),
            pltpu.VMEM((2, 8, 512), F32),
            pltpu.VMEM((2, 2, 512), F32),
            pltpu.VMEM((2, 2, 512), F32),
            pltpu.VMEM((2, 2, 8, 512), F32),
            pltpu.VMEM((3, 2, 2, 512), F32),
            pltpu.VMEM((3, 2, 2, 512), F32),
            pltpu.VMEM((4, 1, 256), F32),
            pltpu.VMEM((2, nx - 1, 1, 256), F32),
            pltpu.VMEM((2, ns - 1, 1, 256), F32),
            dma((16,)),
            dma((4,)),
            dma((9,)),
            dma((2,)),
            dma((3,)),
            dma((8,)),
            dma((8,)),
            dma((4,)),
        ],
        compiler_params=pltpu.CompilerParams(
            collective_id=0, has_side_effects=True, vmem_limit_bytes=24 * 1024 * 1024
        ),
    )
    return call(
        volume.reshape(16, 512),
        footprint.reshape(16, 1024, 256),
        jnp.transpose(tile_block, (0, 2, 3, 1)),
        jnp.transpose(tile_cells, (0, 2, 3, 1)),
        measured,
    )


def solution(mesh):
    ns, nx = mesh.shape["slab"], mesh.shape["xy"]
    placed = (
        P("slab", "xy", None),
        P("slab", "xy", None, None, None, None),
        P("slab", "xy", None, None),
        P("slab", "xy", None, None),
        P(),
    )
    return jax.shard_map(
        functools.partial(body, ns, nx),
        mesh=mesh,
        in_specs=placed,
        out_specs=(P("slab", "xy", None), P(None, ("slab", "xy"))),
        check_vma=False,
    )
```

```python
import functools

import jax
import jax.numpy as jnp
from jax import lax
from jax.experimental import pallas as pl
from jax.experimental.pallas import tpu as pltpu
from jax.sharding import PartitionSpec as P

TV_RATE = 0.8
SMOOTHING = 0.01
MESH = pl.DeviceIdType.MESH
F32 = jnp.float32
BF16 = jnp.bfloat16
GROUPS = 12


def iota(shape, dim):
    return lax.broadcasted_iota(jnp.int32, shape, dim)


def lane_next(x):
    return jnp.where(iota(x.shape, 2) < x.shape[2] - 1, pltpu.roll(x, x.shape[2] - 1, 2), 0.0)


def units(field):
    base = field[:-1]
    diff_a = field[1:] - base
    diff_b = pltpu.roll(base, base.shape[1] - 1, 1) - base
    diff_e = lane_next(base) - base
    inv = lax.rsqrt(diff_a * diff_a + diff_b * diff_b + diff_e * diff_e + SMOOTHING)
    return diff_a * inv, diff_b * inv, diff_e * inv


def tv_slope(field):
    unit_a, unit_b, unit_e = units(field)
    core = field[1:-1]
    prev_b = pltpu.roll(unit_b[1:], 1, 1)
    edge = core * lax.rsqrt(core * core + SMOOTHING)
    prev_e = jnp.where(iota(core.shape, 2) == 0, edge, pltpu.roll(unit_e[1:], 1, 2))
    return unit_a[:-1] + prev_b + prev_e - (unit_a + unit_b + unit_e)[1:]


def lane_partial(x):
    rows = jnp.sum(x, axis=0)
    parts = rows[:, :128]
    for c in range(1, x.shape[2] // 128):
        parts = parts + rows[:, c * 128 : (c + 1) * 128]
    return jnp.sum(parts, axis=0, keepdims=True)


def everyone_else(ns, nx, s, r):
    if (ns, nx) != (16, 8):
        return [(lax.rem(s + d // nx, ns), lax.rem(r + d % nx, nx)) for d in range(1, ns * nx)]
    z = ((s // 2) % 2) * 2 + r // 4
    at_x = [((s // 4 + d) % 4) * 4 for d in range(4)]
    at_z = [(z + d) % 4 for d in range(4)]
    at_y = [(r + d) % 4 for d in range(4)]
    at_core = [(s + d) % 2 for d in range(2)]
    slab_z = [(v // 2) * 2 for v in at_z]
    xy_z = [(v % 2) * 4 for v in at_z]
    slab = {
        (dx, dz, dc): at_x[dx] + slab_z[dz] + at_core[dc] for dx in range(4) for dz in range(4) for dc in range(2)
    }
    xy = {(dz, dy): xy_z[dz] + at_y[dy] for dz in range(4) for dy in range(4)}
    moves = [(dx, dz, dy, dc) for dx in range(4) for dz in range(4) for dy in range(4) for dc in range(2)]
    moves.sort(key=lambda m: -sum(min(d, 4 - d) for d in m[:3]) * 2 - m[3])
    return [(slab[dx, dz, dc], xy[dz, dy]) for dx, dz, dy, dc in moves if (dx, dz, dy, dc) != (0, 0, 0, 0)]


def kernel(
    ns, nx,
    vol_hbm, foot_hbm, blk_hbm, cells_hbm, meas_hbm,
    upd_ref, cor_ref,
    vol, wbuf, blk, cells, meas, bcol, ccol, onehot, contrib,
    send_a, recv_a, total, send_b, recv_b, lhs_b, num, den,
    ublk, rows_lo, rows_hi, uside, hnext, hprev,
    red_s, red_in,
    sem_w, sem_in, sem_s, sem_a, sem_b, sem_c, sem_cs, sem_r,
):
    s = lax.axis_index("slab")
    r = lax.axis_index("xy")
    groups = wbuf.shape[0]
    low_edge = jnp.logical_and(r < 2, s > 0)
    high_edge = jnp.logical_and(r >= nx - 2, s < ns - 1)
    pending = []

    ins = [
        pltpu.make_async_copy(blk_hbm, blk, sem_in.at[0]),
        pltpu.make_async_copy(cells_hbm, cells, sem_in.at[1]),
        pltpu.make_async_copy(vol_hbm, vol, sem_in.at[2]),
        pltpu.make_async_copy(
            meas_hbm.at[:, pl.ds(pl.multiple_of((s * nx + r) * 1024, 1024), 1024)], meas, sem_in.at[3]
        ),
    ]
    for c in ins:
        c.start()

    def load(i):
        return pltpu.make_async_copy(foot_hbm.at[i], wbuf.at[i], sem_w.at[i])

    @pl.loop(0, groups)
    def _(i):
        load(i).start()

    barrier = pltpu.get_barrier_semaphore()

    others = everyone_else(ns, nx, s, r)
    for ds, dr in others:
        pl.semaphore_signal(barrier, inc=1, device_id=(ds, dr), device_id_type=MESH)

    recv_b[GROUPS:] = jnp.zeros((16 - GROUPS,) + recv_b.shape[1:], BF16)

    @pl.when(s == 0)
    def _():
        recv_b[0:2] = jnp.zeros((2,) + recv_b.shape[1:], BF16)
        uside[0] = jnp.zeros(uside.shape[1:], F32)
        hnext[0] = jnp.zeros(hnext.shape[1:], F32)
        hprev[0] = jnp.zeros(hprev.shape[1:], F32)

    @pl.when(s == ns - 1)
    def _():
        recv_b[10:12] = jnp.zeros((2,) + recv_b.shape[1:], BF16)
        uside[1] = jnp.zeros(uside.shape[1:], F32)
        hnext[2] = jnp.zeros(hnext.shape[1:], F32)
        hprev[2] = jnp.zeros(hprev.shape[1:], F32)

    @pl.when(r == 0)
    def _():
        hprev[...] = jnp.zeros(hprev.shape, F32)

    @pl.when(r == nx - 1)
    def _():
        hnext[...] = jnp.zeros(hnext.shape, F32)

    ins[0].wait()
    ins[1].wait()
    for p in range(2):
        for t in range(4):
            bcol[p, 2 * t : 2 * t + 2, 0:8] = blk[p, t]
            ccol[p, 2 * t : 2 * t + 2, 0:8] = cells[p, t]
    lane = iota((8, 128), 1)
    view4 = (iota((8, 128), 0) & 1) * 4
    first = (4 * s - 1) * 8
    for p in range(2):
        blk_p = bcol[p]
        cells_p = ccol[p]
        for x in range(8):
            i = p * 8 + x
            near = jnp.broadcast_to(blk_p[:, x : x + 1], (8, 128)) - first
            target = (near >> 2) * 8 + view4 + (near & 3)
            onehot[i * 8 : i * 8 + 8, :] = jnp.where(lane == target, 1.0, 0.0)
            den[i * 8 : i * 8 + 8, :] = jnp.broadcast_to(cells_p[:, x : x + 1], (8, 128))
    ins[2].wait()

    row16 = iota((16, 128), 0)

    @pl.loop(0, groups)
    def _(i):
        vox = vol[pl.ds(i, 1), :]
        parts = []
        for k in range(8):
            t = k // 2
            spread = jnp.broadcast_to(vox[:, t * 128 : (t + 1) * 128], (16, 128))
            parts.append(
                jnp.where(row16 == k, spread, jnp.where(row16 == k + 8, 1.0, 0.0)).astype(BF16)
            )
        left = jnp.concatenate(parts, axis=1)
        load(i).wait()
        out = jnp.dot(left, wbuf[i], preferred_element_type=F32)
        at = pl.ds(pl.multiple_of(i * 8, 8), 8)
        limit = den[at, :]
        limit = jnp.concatenate([limit, limit], axis=1)
        live = iota((8, 256), 1) < limit
        contrib[at, 0:256] = jnp.where(live, out[0:8], 0.0)
        contrib[at, 256:512] = jnp.where(live, out[8:16], 0.0)

    hot = onehot[...].astype(BF16)
    hot_t = jnp.transpose(onehot[...]).astype(BF16)
    whole = contrib[...]
    high = whole.astype(BF16)
    low = (whole - high.astype(F32)).astype(BF16)
    sums = jnp.dot(hot_t, high, preferred_element_type=F32) + jnp.dot(
        hot_t, low, preferred_element_type=F32
    )
    send_a[...] = sums.reshape(16, 8, 512)

    pl.semaphore_wait(barrier, len(others))

    def remote(src, dst, sem_send, sem_recv, ds, dr):
        return pltpu.make_async_remote_copy(
            src_ref=src, dst_ref=dst, send_sem=sem_send, recv_sem=sem_recv,
            device_id=(ds, dr), device_id_type=MESH,
        )

    @pl.when(s > 0)
    def _():
        for g in range(2):
            remote(send_a.at[g], recv_a.at[nx - 1 + r], sem_s.at[1], sem_a.at[1], s - 1, nx - 2 + g).start()

    @pl.when(s < ns - 1)
    def _():
        for g in range(2):
            remote(send_a.at[10 + g], recv_a.at[nx - 1 + r], sem_s.at[2], sem_a.at[1], s + 1, g).start()

    @pl.loop(1, nx)
    def _(d):
        rp = lax.rem(r + d, nx)
        remote(send_a.at[2 + rp], recv_a.at[d - 1], sem_s.at[0], sem_a.at[0], s, rp).start()

    def sent(ref, sem, cond=None):
        def wait():
            remote(ref, ref, sem, sem_a.at[0], s, r).wait_send()

        pending.append(wait if cond is None else lambda: pl.when(cond)(wait))

    sent(recv_a.at[pl.ds(0, nx - 1)], sem_s.at[0])
    sent(recv_a.at[pl.ds(0, 2)], sem_s.at[1], s > 0)
    sent(recv_a.at[pl.ds(0, 2)], sem_s.at[2], s < ns - 1)
    ins[3].wait()
    m = meas[...]
    seen = jnp.concatenate(
        [m[v : v + 1, q * 256 : (q + 1) * 256] for v in range(2) for q in range(4)], axis=0
    )
    own = send_a[2 + r]
    remote(send_a.at[pl.ds(0, nx - 1)], recv_a.at[pl.ds(0, nx - 1)], sem_s.at[0], sem_a.at[0], s, r).wait_recv()
    total[...] = own + jnp.sum(recv_a[0 : nx - 1], axis=0)

    @pl.when(jnp.logical_or(low_edge, high_edge))
    def _():
        remote(send_a.at[pl.ds(0, nx)], recv_a.at[pl.ds(nx - 1, nx)], sem_s.at[0], sem_a.at[1], s, r).wait_recv()
        total[...] += jnp.sum(recv_a[nx - 1 : 2 * nx - 1], axis=0)

    tot = total[...]
    corr = (seen - tot[:, 0:256]) / jnp.maximum(tot[:, 256:512], 1.0)
    send_b[...] = corr.astype(BF16)
    recv_b[2 + r] = corr.astype(BF16)

    @pl.when(low_edge)
    def _():
        @pl.loop(0, nx)
        def _(rp):
            remote(send_b, recv_b.at[10 + r], sem_s.at[4], sem_b.at[2], s - 1, rp).start()

    @pl.when(high_edge)
    def _():
        @pl.loop(0, nx)
        def _(rp):
            remote(send_b, recv_b.at[r - (nx - 2)], sem_s.at[4], sem_b.at[1], s + 1, rp).start()

    @pl.loop(1, nx)
    def _(d):
        rp = lax.rem(r + d, nx)
        remote(send_b, recv_b.at[2 + r], sem_s.at[3], sem_b.at[0], s, rp).start()

    sent(recv_b.at[pl.ds(0, nx - 1)], sem_s.at[3])
    sent(recv_b.at[pl.ds(0, nx)], sem_s.at[4], jnp.logical_or(low_edge, high_edge))
    for v in range(2):
        for q in range(4):
            cor_ref[v : v + 1, q * 256 : (q + 1) * 256] = corr[v * 4 + q : v * 4 + q + 1, :]

    limit = den[...]
    limit = jnp.concatenate([limit, limit], axis=1)
    live = iota((128, 256), 1) < limit
    live3 = jnp.where(live, 1.0, 0.0).reshape(16, 8, 256)

    remote(recv_b.at[pl.ds(0, nx - 1)], recv_b.at[pl.ds(0, nx - 1)], sem_s.at[3], sem_b.at[0], s, r).wait_recv()

    @pl.when(s > 0)
    def _():
        remote(recv_b.at[pl.ds(0, 2)], recv_b.at[pl.ds(0, 2)], sem_s.at[3], sem_b.at[1], s, r).wait_recv()

    @pl.when(s < ns - 1)
    def _():
        remote(recv_b.at[pl.ds(10, 2)], recv_b.at[pl.ds(10, 2)], sem_s.at[3], sem_b.at[2], s, r).wait_recv()

    table = recv_b[...].astype(F32).reshape(128, 256).astype(BF16)
    picked = jnp.dot(hot, table, preferred_element_type=F32)
    picked = jnp.where(live, picked, 0.0).reshape(16, 8, 256)
    lhs_b[...] = jnp.concatenate([picked, live3], axis=1).astype(BF16)

    row8 = iota((8, 128), 0)

    @pl.loop(0, 2)
    def _(p):
        tops, bottoms = [], []
        for x in range(8):
            i = p * 8 + x
            out = lax.dot_general(
                lhs_b[i], wbuf[i], (((1,), (1,)), ((), ())), preferred_element_type=F32
            )
            for rows, into in ((out[0:8], tops), (out[8:16], bottoms)):
                lanes = []
                for t in range(4):
                    k = 2 * t
                    both = jnp.where(row8 == k, rows[:, k * 128 : k * 128 + 128], 0.0) + jnp.where(
                        row8 == k + 1, rows[:, k * 128 + 128 : k * 128 + 256], 0.0
                    )
                    lanes.append(jnp.sum(both, axis=0, keepdims=True))
                into.append(jnp.concatenate(lanes, axis=1))
        num[pl.ds(pl.multiple_of(p * 8, 8), 8), :] = jnp.concatenate(tops, axis=0)
        num[pl.ds(pl.multiple_of(p * 8 + 16, 8), 8), :] = jnp.concatenate(bottoms, axis=0)

    before = vol[...]
    sart = jnp.maximum(before + num[0:groups] / num[groups : 2 * groups], 0.0)
    gap = (sart - before).reshape(2, 8, 512)
    cells3 = sart.reshape(2, 8, 512)

    ublk[...] = cells3
    rows_lo[...] = cells3[:, 0:2, :]
    rows_hi[...] = cells3[:, 6:8, :]

    def exists(ds, dr):
        ok = None
        for cond in (
            [s > 0] if ds < 0 else [s < ns - 1] if ds > 0 else []
        ) + ([r > 0] if dr < 0 else [r < nx - 1] if dr > 0 else []):
            ok = cond if ok is None else jnp.logical_and(ok, cond)
        return ok

    def halo(n, ds, dr):
        if dr == 0:
            src, dst = ublk, uside.at[1 if ds < 0 else 0]
        elif dr < 0:
            src, dst = rows_lo, hnext.at[1 - ds]
        else:
            src, dst = rows_hi, hprev.at[1 - ds]
        return remote(src, dst, sem_cs.at[n], sem_c.at[n], s + ds, r + dr)

    offsets = [(ds, dr) for ds in (-1, 1) for dr in (-1, 1, 0)] + [(0, -1), (0, 1)]
    for n, (ds, dr) in enumerate(offsets):

        @pl.when(exists(ds, dr))
        def _():
            halo(n, ds, dr).start()

        pending.append(
            lambda n=n, ds=ds, dr=dr: pl.when(exists(ds, dr))(lambda: halo(n, ds, dr).wait_send())
        )

    for n, (ds, dr) in enumerate(offsets):

        @pl.when(exists(-ds, -dr))
        def _():
            halo(n, ds, dr).wait_recv()

    def padded(main, after, before):
        return jnp.concatenate([main, after, jnp.zeros((4, 512), F32), before], axis=0)[None]

    field = jnp.concatenate(
        [padded(uside[0, p], hnext[0, p], hprev[0, p]) for p in range(2)]
        + [padded(ublk[p], hnext[1, p], hprev[1, p]) for p in range(2)]
        + [padded(uside[1, p], hnext[2, p], hprev[2, p]) for p in range(2)],
        axis=0,
    )
    slope = tv_slope(field)

    def reduce_all(n, parts):
        red_s[n] = parts
        for j, (ds, dr) in enumerate(others):
            remote(red_s.at[n], red_in.at[n, j], sem_s.at[5 + n], sem_r.at[n], ds, dr).start()
        sent(red_in.at[n], sem_s.at[5 + n])
        remote(red_in.at[n], red_in.at[n], sem_s.at[5 + n], sem_r.at[n], s, r).wait_recv()
        return parts + jnp.sum(red_in[n], axis=0)

    def half(x):
        return x + pltpu.roll(x, 64, 1)

    own_slope = slope[1:3, 0:8, :]
    left = iota((1, 128), 1) < 64
    both = reduce_all(
        0, jnp.where(left, half(lane_partial(gap * gap)), half(lane_partial(own_slope * own_slope)))
    )
    rate = TV_RATE * jnp.sqrt(jnp.sum(jnp.where(left, both, 0.0), axis=1, keepdims=True))
    scale = jnp.sqrt(jnp.sum(jnp.where(left, 0.0, both), axis=1, keepdims=True) + 1e-06)
    inner = field[1:5]
    plane = iota(inner.shape, 0) + jnp.where(s > 0, 1, 0)
    row = iota(inner.shape, 1)
    inside = jnp.logical_and(plane >= 1, iota(inner.shape, 0) < jnp.where(s < ns - 1, 4, 3))
    inside = jnp.logical_and(inside, row < jnp.where(r > 0, 16, 12))
    inside = jnp.logical_and(inside, jnp.logical_or(row < 8, jnp.logical_or(row >= 12, r < nx - 1)))
    step = (rate / scale).reshape(1, 1, 1)
    first_u = jnp.where(inside, inner - step * slope, 0.0)
    slope2 = tv_slope(first_u)[:, 0:8, :]
    both2 = reduce_all(1, lane_partial(slope2 * slope2))
    scale2 = jnp.sqrt(jnp.sum(both2, axis=1, keepdims=True) + 1e-06)
    step2 = (rate / scale2).reshape(1, 1, 1)
    upd_ref[...] = first_u[1:3, 0:8, :] - step2 * slope2

    for wait in pending:
        wait()


def body(ns, nx, volume, footprint, tile_block, tile_cells, measured):
    any_space = pl.BlockSpec(memory_space=pltpu.HBM)
    vmem = pl.BlockSpec(memory_space=pltpu.VMEM)
    dma = pltpu.SemaphoreType.DMA
    call = pl.pallas_call(
        functools.partial(kernel, ns, nx),
        out_shape=(
            jax.ShapeDtypeStruct((2, 8, 512), F32),
            jax.ShapeDtypeStruct((2, 1024), F32),
        ),
        in_specs=[any_space] * 5,
        out_specs=(vmem, vmem),
        scratch_shapes=[
            pltpu.VMEM((16, 512), F32),
            pltpu.VMEM((16, 1024, 256), BF16),
            pltpu.VMEM((2, 4, 2, 8), jnp.int32),
            pltpu.VMEM((2, 4, 2, 8), jnp.int32),
            pltpu.VMEM((2, 1024), F32),
            pltpu.VMEM((2, 8, 128), jnp.int32),
            pltpu.VMEM((2, 8, 128), jnp.int32),
            pltpu.VMEM((128, 128), F32),
            pltpu.VMEM((128, 512), F32),
            pltpu.VMEM((16, 8, 512), F32),
            pltpu.VMEM((2 * nx - 1, 8, 512), F32),
            pltpu.VMEM((8, 512), F32),
            pltpu.VMEM((8, 256), BF16),
            pltpu.VMEM((16, 8, 256), BF16),
            pltpu.VMEM((16, 16, 256), BF16),
            pltpu.VMEM((32, 512), F32),
            pltpu.VMEM((128, 128), jnp.int32),
            pltpu.VMEM((2, 8, 512), F32),
            pltpu.VMEM((2, 2, 512), F32),
            pltpu.VMEM((2, 2, 512), F32),
            pltpu.VMEM((2, 2, 8, 512), F32),
            pltpu.VMEM((3, 2, 2, 512), F32),
            pltpu.VMEM((3, 2, 2, 512), F32),
            pltpu.VMEM((2, 1, 128), F32),
            pltpu.VMEM((2, ns * nx - 1, 1, 128), F32),
            dma((16,)),
            dma((4,)),
            dma((7,)),
            dma((2,)),
            dma((3,)),
            dma((8,)),
            dma((8,)),
            dma((2,)),
        ],
        compiler_params=pltpu.CompilerParams(
            collective_id=0, has_side_effects=True, vmem_limit_bytes=60 * 1024 * 1024
        ),
    )
    return call(
        volume.reshape(16, 512),
        footprint.reshape(16, 1024, 256),
        jnp.transpose(tile_block, (0, 2, 3, 1)),
        jnp.transpose(tile_cells, (0, 2, 3, 1)),
        measured,
    )


def solution(mesh):
    ns, nx = mesh.shape["slab"], mesh.shape["xy"]
    placed = (
        P("slab", "xy", None),
        P("slab", "xy", None, None, None, None),
        P("slab", "xy", None, None),
        P("slab", "xy", None, None),
        P(),
    )
    return jax.shard_map(
        functools.partial(body, ns, nx),
        mesh=mesh,
        in_specs=placed,
        out_specs=(P("slab", "xy", None), P(None, ("slab", "xy"))),
        check_vma=False,
    )
```

```python
import functools

import jax
import jax.numpy as jnp
from jax import lax
from jax.experimental import pallas as pl
from jax.experimental.pallas import tpu as pltpu
from jax.sharding import PartitionSpec as P

TV_RATE = 0.8
SMOOTHING = 0.01
MESH = pl.DeviceIdType.MESH
F32 = jnp.float32
BF16 = jnp.bfloat16
GROUPS = 12


def iota(shape, dim):
    return lax.broadcasted_iota(jnp.int32, shape, dim)


def lane_next(x):
    return jnp.where(iota(x.shape, 2) < x.shape[2] - 1, pltpu.roll(x, x.shape[2] - 1, 2), 0.0)


def units(field):
    base = field[:-1]
    diff_a = field[1:] - base
    diff_b = pltpu.roll(base, base.shape[1] - 1, 1) - base
    diff_e = lane_next(base) - base
    inv = lax.rsqrt(diff_a * diff_a + diff_b * diff_b + diff_e * diff_e + SMOOTHING)
    return diff_a * inv, diff_b * inv, diff_e * inv


def tv_slope(field):
    unit_a, unit_b, unit_e = units(field)
    core = field[1:-1]
    prev_b = pltpu.roll(unit_b[1:], 1, 1)
    edge = core * lax.rsqrt(core * core + SMOOTHING)
    prev_e = jnp.where(iota(core.shape, 2) == 0, edge, pltpu.roll(unit_e[1:], 1, 2))
    return unit_a[:-1] + prev_b + prev_e - (unit_a + unit_b + unit_e)[1:]


def lane_partial(x):
    rows = jnp.sum(x, axis=0)
    parts = rows[:, :128]
    for c in range(1, x.shape[2] // 128):
        parts = parts + rows[:, c * 128 : (c + 1) * 128]
    return jnp.sum(parts, axis=0, keepdims=True)


def everyone_else(ns, nx, s, r):
    if (ns, nx) != (16, 8):
        return [(lax.rem(s + d // nx, ns), lax.rem(r + d % nx, nx)) for d in range(1, ns * nx)]
    z = ((s // 2) % 2) * 2 + r // 4
    at_x = [((s // 4 + d) % 4) * 4 for d in range(4)]
    at_z = [(z + d) % 4 for d in range(4)]
    at_y = [(r + d) % 4 for d in range(4)]
    at_core = [(s + d) % 2 for d in range(2)]
    slab_z = [(v // 2) * 2 for v in at_z]
    xy_z = [(v % 2) * 4 for v in at_z]
    slab = {
        (dx, dz, dc): at_x[dx] + slab_z[dz] + at_core[dc] for dx in range(4) for dz in range(4) for dc in range(2)
    }
    xy = {(dz, dy): xy_z[dz] + at_y[dy] for dz in range(4) for dy in range(4)}
    moves = [(dx, dz, dy, dc) for dx in range(4) for dz in range(4) for dy in range(4) for dc in range(2)]
    moves.sort(key=lambda m: -sum(min(d, 4 - d) for d in m[:3]) * 2 - m[3])
    return [(slab[dx, dz, dc], xy[dz, dy]) for dx, dz, dy, dc in moves if (dx, dz, dy, dc) != (0, 0, 0, 0)]


def kernel(
    ns, nx,
    vol_hbm, foot_hbm, blk_hbm, cells_hbm, meas_hbm,
    upd_ref, cor_ref,
    vol, wbuf, blk, cells, meas, bcol, ccol, onehot, contrib,
    send_a, recv_a, total, send_b, recv_b, lhs_b, num, den,
    ublk, rows_lo, rows_hi, uside, hnext, hprev,
    red_s, red_in,
    sem_w, sem_in, sem_s, sem_a, sem_b, sem_c, sem_cs, sem_r,
):
    s = lax.axis_index("slab")
    r = lax.axis_index("xy")
    groups = wbuf.shape[0]
    low_edge = jnp.logical_and(r < 2, s > 0)
    high_edge = jnp.logical_and(r >= nx - 2, s < ns - 1)
    pending = []

    ins = [
        pltpu.make_async_copy(blk_hbm, blk, sem_in.at[0]),
        pltpu.make_async_copy(cells_hbm, cells, sem_in.at[1]),
        pltpu.make_async_copy(vol_hbm, vol, sem_in.at[2]),
        pltpu.make_async_copy(
            meas_hbm.at[:, pl.ds(pl.multiple_of((s * nx + r) * 1024, 1024), 1024)], meas, sem_in.at[3]
        ),
    ]
    for c in ins:
        c.start()

    def load(i):
        return pltpu.make_async_copy(foot_hbm.at[i], wbuf.at[i], sem_w.at[i])

    @pl.loop(0, groups)
    def _(i):
        load(i).start()

    barrier = pltpu.get_barrier_semaphore()

    others = everyone_else(ns, nx, s, r)
    for ds, dr in others:
        pl.semaphore_signal(barrier, inc=1, device_id=(ds, dr), device_id_type=MESH)

    recv_b[GROUPS:] = jnp.zeros((16 - GROUPS,) + recv_b.shape[1:], BF16)

    @pl.when(s == 0)
    def _():
        recv_b[0:2] = jnp.zeros((2,) + recv_b.shape[1:], BF16)
        uside[0] = jnp.zeros(uside.shape[1:], F32)
        hnext[0] = jnp.zeros(hnext.shape[1:], F32)
        hprev[0] = jnp.zeros(hprev.shape[1:], F32)

    @pl.when(s == ns - 1)
    def _():
        recv_b[10:12] = jnp.zeros((2,) + recv_b.shape[1:], BF16)
        uside[1] = jnp.zeros(uside.shape[1:], F32)
        hnext[2] = jnp.zeros(hnext.shape[1:], F32)
        hprev[2] = jnp.zeros(hprev.shape[1:], F32)

    @pl.when(r == 0)
    def _():
        hprev[...] = jnp.zeros(hprev.shape, F32)

    @pl.when(r == nx - 1)
    def _():
        hnext[...] = jnp.zeros(hnext.shape, F32)

    ins[0].wait()
    ins[1].wait()
    for p in range(2):
        for t in range(4):
            bcol[p, 2 * t : 2 * t + 2, 0:8] = blk[p, t]
            ccol[p, 2 * t : 2 * t + 2, 0:8] = cells[p, t]
    lane = iota((8, 128), 1)
    view4 = (iota((8, 128), 0) & 1) * 4
    first = (4 * s - 1) * 8
    for p in range(2):
        blk_p = bcol[p]
        cells_p = ccol[p]
        for x in range(8):
            i = p * 8 + x
            near = jnp.broadcast_to(blk_p[:, x : x + 1], (8, 128)) - first
            target = (near >> 2) * 8 + view4 + (near & 3)
            onehot[i * 8 : i * 8 + 8, :] = jnp.where(lane == target, 1.0, 0.0)
            den[i * 8 : i * 8 + 8, :] = jnp.broadcast_to(cells_p[:, x : x + 1], (8, 128))
    ins[2].wait()

    row16 = iota((16, 128), 0)

    @pl.loop(0, groups)
    def _(i):
        vox = vol[pl.ds(i, 1), :]
        parts = []
        for k in range(8):
            t = k // 2
            spread = jnp.broadcast_to(vox[:, t * 128 : (t + 1) * 128], (16, 128))
            parts.append(
                jnp.where(row16 == k, spread, jnp.where(row16 == k + 8, 1.0, 0.0)).astype(BF16)
            )
        left = jnp.concatenate(parts, axis=1)
        load(i).wait()
        out = jnp.dot(left, wbuf[i], preferred_element_type=F32)
        at = pl.ds(pl.multiple_of(i * 8, 8), 8)
        limit = den[at, :]
        limit = jnp.concatenate([limit, limit], axis=1)
        live = iota((8, 256), 1) < limit
        contrib[at, 0:256] = jnp.where(live, out[0:8], 0.0)
        contrib[at, 256:512] = jnp.where(live, out[8:16], 0.0)

    hot = onehot[...].astype(BF16)
    hot_t = jnp.transpose(onehot[...]).astype(BF16)
    whole = contrib[...]
    high = whole.astype(BF16)
    low = (whole - high.astype(F32)).astype(BF16)
    sums = jnp.dot(hot_t, high, preferred_element_type=F32) + jnp.dot(
        hot_t, low, preferred_element_type=F32
    )
    send_a[...] = sums.reshape(16, 8, 512)

    pl.semaphore_wait(barrier, len(others))

    def remote(src, dst, sem_send, sem_recv, ds, dr):
        return pltpu.make_async_remote_copy(
            src_ref=src, dst_ref=dst, send_sem=sem_send, recv_sem=sem_recv,
            device_id=(ds, dr), device_id_type=MESH,
        )

    @pl.when(s > 0)
    def _():
        for g in range(2):
            remote(send_a.at[g], recv_a.at[nx - 1 + r], sem_s.at[1], sem_a.at[1], s - 1, nx - 2 + g).start()

    @pl.when(s < ns - 1)
    def _():
        for g in range(2):
            remote(send_a.at[10 + g], recv_a.at[nx - 1 + r], sem_s.at[2], sem_a.at[1], s + 1, g).start()

    @pl.loop(1, nx)
    def _(d):
        rp = lax.rem(r + d, nx)
        remote(send_a.at[2 + rp], recv_a.at[d - 1], sem_s.at[0], sem_a.at[0], s, rp).start()

    def sent(ref, sem, cond=None):
        def wait():
            remote(ref, ref, sem, sem_a.at[0], s, r).wait_send()

        pending.append(wait if cond is None else lambda: pl.when(cond)(wait))

    sent(recv_a.at[pl.ds(0, nx - 1)], sem_s.at[0])
    sent(recv_a.at[pl.ds(0, 2)], sem_s.at[1], s > 0)
    sent(recv_a.at[pl.ds(0, 2)], sem_s.at[2], s < ns - 1)
    ins[3].wait()
    m = meas[...]
    seen = jnp.concatenate(
        [m[v : v + 1, q * 256 : (q + 1) * 256] for v in range(2) for q in range(4)], axis=0
    )
    own = send_a[2 + r]
    remote(send_a.at[pl.ds(0, nx - 1)], recv_a.at[pl.ds(0, nx - 1)], sem_s.at[0], sem_a.at[0], s, r).wait_recv()
    total[...] = own + jnp.sum(recv_a[0 : nx - 1], axis=0)

    @pl.when(jnp.logical_or(low_edge, high_edge))
    def _():
        remote(send_a.at[pl.ds(0, nx)], recv_a.at[pl.ds(nx - 1, nx)], sem_s.at[0], sem_a.at[1], s, r).wait_recv()
        total[...] += jnp.sum(recv_a[nx - 1 : 2 * nx - 1], axis=0)

    tot = total[...]
    corr = (seen - tot[:, 0:256]) / jnp.maximum(tot[:, 256:512], 1.0)
    send_b[...] = corr.astype(BF16)
    recv_b[2 + r] = corr.astype(BF16)

    @pl.when(low_edge)
    def _():
        @pl.loop(0, nx)
        def _(rp):
            remote(send_b, recv_b.at[10 + r], sem_s.at[4], sem_b.at[2], s - 1, rp).start()

    @pl.when(high_edge)
    def _():
        @pl.loop(0, nx)
        def _(rp):
            remote(send_b, recv_b.at[r - (nx - 2)], sem_s.at[4], sem_b.at[1], s + 1, rp).start()

    @pl.loop(1, nx)
    def _(d):
        rp = lax.rem(r + d, nx)
        remote(send_b, recv_b.at[2 + r], sem_s.at[3], sem_b.at[0], s, rp).start()

    sent(recv_b.at[pl.ds(0, nx - 1)], sem_s.at[3])
    sent(recv_b.at[pl.ds(0, nx)], sem_s.at[4], jnp.logical_or(low_edge, high_edge))
    for v in range(2):
        for q in range(4):
            cor_ref[v : v + 1, q * 256 : (q + 1) * 256] = corr[v * 4 + q : v * 4 + q + 1, :]

    limit = den[...]
    limit = jnp.concatenate([limit, limit], axis=1)
    live = iota((128, 256), 1) < limit
    live3 = jnp.where(live, 1.0, 0.0).reshape(16, 8, 256)

    remote(recv_b.at[pl.ds(0, nx - 1)], recv_b.at[pl.ds(0, nx - 1)], sem_s.at[3], sem_b.at[0], s, r).wait_recv()

    @pl.when(s > 0)
    def _():
        remote(recv_b.at[pl.ds(0, 2)], recv_b.at[pl.ds(0, 2)], sem_s.at[3], sem_b.at[1], s, r).wait_recv()

    @pl.when(s < ns - 1)
    def _():
        remote(recv_b.at[pl.ds(10, 2)], recv_b.at[pl.ds(10, 2)], sem_s.at[3], sem_b.at[2], s, r).wait_recv()

    table = recv_b[...].astype(F32).reshape(128, 256).astype(BF16)
    picked = jnp.dot(hot, table, preferred_element_type=F32)
    picked = jnp.where(live, picked, 0.0).reshape(16, 8, 256)
    lhs_b[...] = jnp.concatenate([picked, live3], axis=1).astype(BF16)

    row8 = iota((8, 128), 0)

    @pl.loop(0, 2)
    def _(p):
        tops, bottoms = [], []
        for x in range(8):
            i = p * 8 + x
            out = lax.dot_general(
                lhs_b[i], wbuf[i], (((1,), (1,)), ((), ())), preferred_element_type=F32
            )
            for rows, into in ((out[0:8], tops), (out[8:16], bottoms)):
                lanes = []
                for t in range(4):
                    k = 2 * t
                    both = jnp.where(row8 == k, rows[:, k * 128 : k * 128 + 128], 0.0) + jnp.where(
                        row8 == k + 1, rows[:, k * 128 + 128 : k * 128 + 256], 0.0
                    )
                    lanes.append(jnp.sum(both, axis=0, keepdims=True))
                into.append(jnp.concatenate(lanes, axis=1))
        num[pl.ds(pl.multiple_of(p * 8, 8), 8), :] = jnp.concatenate(tops, axis=0)
        num[pl.ds(pl.multiple_of(p * 8 + 16, 8), 8), :] = jnp.concatenate(bottoms, axis=0)

    before = vol[...]
    sart = jnp.maximum(before + num[0:groups] / num[groups : 2 * groups], 0.0)
    gap = (sart - before).reshape(2, 8, 512)
    cells3 = sart.reshape(2, 8, 512)

    ublk[...] = cells3
    rows_lo[...] = cells3[:, 0:2, :]
    rows_hi[...] = cells3[:, 6:8, :]

    def exists(ds, dr):
        ok = None
        for cond in (
            [s > 0] if ds < 0 else [s < ns - 1] if ds > 0 else []
        ) + ([r > 0] if dr < 0 else [r < nx - 1] if dr > 0 else []):
            ok = cond if ok is None else jnp.logical_and(ok, cond)
        return ok

    def halo(n, ds, dr):
        if dr == 0:
            src, dst = ublk, uside.at[1 if ds < 0 else 0]
        elif dr < 0:
            src, dst = rows_lo, hnext.at[1 - ds]
        else:
            src, dst = rows_hi, hprev.at[1 - ds]
        return remote(src, dst, sem_cs.at[n], sem_c.at[n], s + ds, r + dr)

    offsets = [(ds, dr) for ds in (-1, 1) for dr in (-1, 1, 0)] + [(0, -1), (0, 1)]
    for n, (ds, dr) in enumerate(offsets):

        @pl.when(exists(ds, dr))
        def _():
            halo(n, ds, dr).start()

        pending.append(
            lambda n=n, ds=ds, dr=dr: pl.when(exists(ds, dr))(lambda: halo(n, ds, dr).wait_send())
        )

    for n, (ds, dr) in enumerate(offsets):

        @pl.when(exists(-ds, -dr))
        def _():
            halo(n, ds, dr).wait_recv()

    def padded(main, after, before):
        return jnp.concatenate([main, after, jnp.zeros((4, 512), F32), before], axis=0)[None]

    field = jnp.concatenate(
        [padded(uside[0, p], hnext[0, p], hprev[0, p]) for p in range(2)]
        + [padded(ublk[p], hnext[1, p], hprev[1, p]) for p in range(2)]
        + [padded(uside[1, p], hnext[2, p], hprev[2, p]) for p in range(2)],
        axis=0,
    )
    slope = tv_slope(field)

    def reduce_all(n, parts):
        red_s[n] = parts
        for j, (ds, dr) in enumerate(others):
            remote(red_s.at[n], red_in.at[n, j], sem_s.at[5 + n], sem_r.at[n], ds, dr).start()
        sent(red_in.at[n], sem_s.at[5 + n])
        remote(red_in.at[n], red_in.at[n], sem_s.at[5 + n], sem_r.at[n], s, r).wait_recv()
        return parts + jnp.sum(red_in[n], axis=0)

    def half(x):
        return x + pltpu.roll(x, 64, 1)

    own_slope = slope[1:3, 0:8, :]
    left = iota((1, 128), 1) < 64
    both = reduce_all(
        0, jnp.where(left, half(lane_partial(gap * gap)), half(lane_partial(own_slope * own_slope)))
    )
    rate = TV_RATE * jnp.sqrt(jnp.sum(jnp.where(left, both, 0.0), axis=1, keepdims=True))
    scale = jnp.sqrt(jnp.sum(jnp.where(left, 0.0, both), axis=1, keepdims=True) + 1e-06)
    inner = field[1:5]
    plane = iota(inner.shape, 0) + jnp.where(s > 0, 1, 0)
    row = iota(inner.shape, 1)
    inside = jnp.logical_and(plane >= 1, iota(inner.shape, 0) < jnp.where(s < ns - 1, 4, 3))
    inside = jnp.logical_and(inside, row < jnp.where(r > 0, 16, 12))
    inside = jnp.logical_and(inside, jnp.logical_or(row < 8, jnp.logical_or(row >= 12, r < nx - 1)))
    step = (rate / scale).reshape(1, 1, 1)
    first_u = jnp.where(inside, inner - step * slope, 0.0)
    slope2 = tv_slope(first_u)[:, 0:8, :]
    both2 = reduce_all(1, lane_partial(slope2 * slope2))
    scale2 = jnp.sqrt(jnp.sum(both2, axis=1, keepdims=True) + 1e-06)
    step2 = (rate / scale2).reshape(1, 1, 1)
    upd_ref[...] = first_u[1:3, 0:8, :] - step2 * slope2

    for wait in pending:
        wait()


def put_out(upd, cor, upd_hbm, cor_hbm, sem):
    copies = [pltpu.make_async_copy(upd, upd_hbm, sem.at[0]), pltpu.make_async_copy(cor, cor_hbm, sem.at[1])]
    for c in copies:
        c.start()
    for c in copies:
        c.wait()


def body(ns, nx, volume, footprint, tile_block, tile_cells, measured):
    any_space = pl.BlockSpec(memory_space=pltpu.HBM)
    vmem = pl.BlockSpec(memory_space=pltpu.VMEM)
    dma = pltpu.SemaphoreType.DMA
    call = pl.pallas_call(
        functools.partial(kernel, ns, nx),
        out_shape=(pltpu.VMEM((2, 8, 512), F32), pltpu.VMEM((2, 1024), F32)),
        in_specs=[any_space] * 5,
        out_specs=(vmem, vmem),
        scratch_shapes=[
            pltpu.VMEM((16, 512), F32),
            pltpu.VMEM((16, 1024, 256), BF16),
            pltpu.VMEM((2, 4, 2, 8), jnp.int32),
            pltpu.VMEM((2, 4, 2, 8), jnp.int32),
            pltpu.VMEM((2, 1024), F32),
            pltpu.VMEM((2, 8, 128), jnp.int32),
            pltpu.VMEM((2, 8, 128), jnp.int32),
            pltpu.VMEM((128, 128), F32),
            pltpu.VMEM((128, 512), F32),
            pltpu.VMEM((16, 8, 512), F32),
            pltpu.VMEM((2 * nx - 1, 8, 512), F32),
            pltpu.VMEM((8, 512), F32),
            pltpu.VMEM((8, 256), BF16),
            pltpu.VMEM((16, 8, 256), BF16),
            pltpu.VMEM((16, 16, 256), BF16),
            pltpu.VMEM((32, 512), F32),
            pltpu.VMEM((128, 128), jnp.int32),
            pltpu.VMEM((2, 8, 512), F32),
            pltpu.VMEM((2, 2, 512), F32),
            pltpu.VMEM((2, 2, 512), F32),
            pltpu.VMEM((2, 2, 8, 512), F32),
            pltpu.VMEM((3, 2, 2, 512), F32),
            pltpu.VMEM((3, 2, 2, 512), F32),
            pltpu.VMEM((2, 1, 128), F32),
            pltpu.VMEM((2, ns * nx - 1, 1, 128), F32),
            dma((16,)),
            dma((4,)),
            dma((7,)),
            dma((2,)),
            dma((3,)),
            dma((8,)),
            dma((8,)),
            dma((2,)),
        ],
        compiler_params=pltpu.CompilerParams(
            collective_id=0, has_side_effects=True, vmem_limit_bytes=60 * 1024 * 1024
        ),
    )
    operands = (
        volume.reshape(16, 512),
        footprint.reshape(16, 1024, 256),
        jnp.transpose(tile_block, (0, 2, 3, 1)),
        jnp.transpose(tile_cells, (0, 2, 3, 1)),
        measured,
    )
    results = call(*[pltpu.with_memory_space_constraint(x, pltpu.HBM) for x in operands])
    return pl.pallas_call(
        put_out,
        out_shape=tuple(jax.ShapeDtypeStruct(x.shape, F32) for x in results),
        in_specs=[vmem, vmem],
        out_specs=(any_space, any_space),
        scratch_shapes=[dma((2,))],
        compiler_params=pltpu.CompilerParams(vmem_limit_bytes=1024 * 1024),
    )(*[pltpu.with_memory_space_constraint(x, pltpu.VMEM) for x in results])


def solution(mesh):
    ns, nx = mesh.shape["slab"], mesh.shape["xy"]
    placed = (
        P("slab", "xy", None),
        P("slab", "xy", None, None, None, None),
        P("slab", "xy", None, None),
        P("slab", "xy", None, None),
        P(),
    )
    return jax.shard_map(
        functools.partial(body, ns, nx),
        mesh=mesh,
        in_specs=placed,
        out_specs=(P("slab", "xy", None), P(None, ("slab", "xy"))),
        check_vma=False,
    )
```

```python
import functools

import jax
import jax.numpy as jnp
from jax import lax
from jax.experimental import pallas as pl
from jax.experimental.pallas import tpu as pltpu
from jax.sharding import PartitionSpec as P

TV_RATE = 0.8
SMOOTHING = 0.01
MESH = pl.DeviceIdType.MESH
F32 = jnp.float32
BF16 = jnp.bfloat16
PIECES = ((0, 4), (4, 8), (8, 12), (12, 16))
GROUPS = 12


def iota(shape, dim):
    return lax.broadcasted_iota(jnp.int32, shape, dim)


def lane_next(x):
    return jnp.where(iota(x.shape, 2) < x.shape[2] - 1, pltpu.roll(x, x.shape[2] - 1, 2), 0.0)


def units(field):
    base = field[:-1]
    diff_a = field[1:] - base
    diff_b = pltpu.roll(base, base.shape[1] - 1, 1) - base
    diff_e = lane_next(base) - base
    inv = lax.rsqrt(diff_a * diff_a + diff_b * diff_b + diff_e * diff_e + SMOOTHING)
    return diff_a * inv, diff_b * inv, diff_e * inv


def tv_slope(field):
    unit_a, unit_b, unit_e = units(field)
    core = field[1:-1]
    prev_b = pltpu.roll(unit_b[1:], 1, 1)
    edge = core * lax.rsqrt(core * core + SMOOTHING)
    prev_e = jnp.where(iota(core.shape, 2) == 0, edge, pltpu.roll(unit_e[1:], 1, 2))
    return unit_a[:-1] + prev_b + prev_e - (unit_a + unit_b + unit_e)[1:]


def lane_partial(x):
    rows = jnp.sum(x, axis=0)
    parts = rows[:, :128]
    for c in range(1, x.shape[2] // 128):
        parts = parts + rows[:, c * 128 : (c + 1) * 128]
    return jnp.sum(parts, axis=0, keepdims=True)


def everyone_else(ns, nx, s, r):
    if (ns, nx) != (16, 8):
        return [(lax.rem(s + d // nx, ns), lax.rem(r + d % nx, nx)) for d in range(1, ns * nx)]
    z = ((s // 2) % 2) * 2 + r // 4
    at_x = [((s // 4 + d) % 4) * 4 for d in range(4)]
    at_z = [(z + d) % 4 for d in range(4)]
    at_y = [(r + d) % 4 for d in range(4)]
    at_core = [(s + d) % 2 for d in range(2)]
    slab_z = [(v // 2) * 2 for v in at_z]
    xy_z = [(v % 2) * 4 for v in at_z]
    slab = {
        (dx, dz, dc): at_x[dx] + slab_z[dz] + at_core[dc] for dx in range(4) for dz in range(4) for dc in range(2)
    }
    xy = {(dz, dy): xy_z[dz] + at_y[dy] for dz in range(4) for dy in range(4)}
    moves = [(dx, dz, dy, dc) for dx in range(4) for dz in range(4) for dy in range(4) for dc in range(2)]
    moves.sort(key=lambda m: -sum(min(d, 4 - d) for d in m[:3]) * 2 - m[3])
    return [(slab[dx, dz, dc], xy[dz, dy]) for dx, dz, dy, dc in moves if (dx, dz, dy, dc) != (0, 0, 0, 0)]


def kernel(
    ns, nx,
    vol_hbm, foot_hbm, blk_hbm, cells_hbm, meas_hbm,
    upd_ref, cor_ref,
    vol, wbuf, blk, cells, meas, bcol, ccol, onehot, onehot_t, contrib,
    send_a, recv_a, total, send_b, recv_b, lhs_b, num, den,
    ublk, uside, halo,
    red_s, red_in,
    sem_w, sem_in, sem_s, sem_a, sem_b, sem_c, sem_cs, sem_r, sem_k,
):
    s = lax.axis_index("slab")
    r = lax.axis_index("xy")
    groups = wbuf.shape[0]
    low_edge = jnp.logical_and(r < 2, s > 0)
    high_edge = jnp.logical_and(r >= nx - 2, s < ns - 1)
    pending = []

    ins = [
        pltpu.make_async_copy(blk_hbm, blk, sem_in.at[0]),
        pltpu.make_async_copy(cells_hbm, cells, sem_in.at[1]),
        pltpu.make_async_copy(vol_hbm, vol, sem_in.at[2]),
        pltpu.make_async_copy(
            meas_hbm.at[:, pl.ds(pl.multiple_of((s * nx + r) * 1024, 1024), 1024)], meas, sem_in.at[3]
        ),
    ]
    for c in ins:
        c.start()

    def load(n):
        first, last = PIECES[n]
        at = pl.ds(first, last - first)
        return pltpu.make_async_copy(foot_hbm.at[at], wbuf.at[at], sem_w.at[n])

    for n in range(len(PIECES)):
        load(n).start()

    barrier = pltpu.get_barrier_semaphore()

    def hello(ds, dr):
        pl.semaphore_signal(barrier, inc=1, device_id=(ds, dr), device_id_type=MESH)

    recv_b[...] = jnp.zeros(recv_b.shape, BF16)
    uside[...] = jnp.zeros(uside.shape, F32)
    halo[...] = jnp.zeros(halo.shape, F32)

    @pl.when(s > 0)
    def _():
        for d in range(nx):
            hello(s - 1, d)

    @pl.when(s < ns - 1)
    def _():
        for d in range(nx):
            hello(s + 1, d)

    for d in range(1, nx):
        hello(s, lax.rem(r + d, nx))

    ins[0].wait()
    ins[1].wait()
    for p in range(2):
        for t in range(4):
            bcol[p, 2 * t : 2 * t + 2, 0:8] = blk[p, t]
            ccol[p, 2 * t : 2 * t + 2, 0:8] = cells[p, t]
    lane = iota((8, 128), 1)
    view4 = (iota((8, 128), 0) & 1) * 4
    first = (4 * s - 1) * 8
    hots = []
    for p in range(2):
        blk_p = bcol[p]
        cells_p = ccol[p]
        for x in range(8):
            i = p * 8 + x
            near = jnp.broadcast_to(blk_p[:, x : x + 1], (8, 128)) - first
            target = (near >> 2) * 8 + view4 + (near & 3)
            hots.append(jnp.where(lane == target, 1.0, 0.0))
            den[i * 8 : i * 8 + 8, :] = jnp.broadcast_to(cells_p[:, x : x + 1], (8, 128))
    hot = jnp.concatenate(hots, axis=0)
    onehot[...] = hot.astype(BF16)
    hot = jnp.transpose(hot).astype(BF16)
    onehot_t[...] = jnp.concatenate([hot, hot], axis=1)
    ins[2].wait()

    row16 = iota((16, 128), 0)

    @pl.loop(0, groups // 2)
    def _(pair):
        both = []
        for n, (begin, _) in enumerate(PIECES):

            @pl.when(pair * 2 == begin)
            def _(n=n):
                load(n).wait()

        for h in range(2):
            i = pair * 2 + h
            vox = vol[pl.ds(i, 1), :]
            parts = []
            for k in range(8):
                t = k // 2
                spread = jnp.broadcast_to(vox[:, t * 128 : (t + 1) * 128], (16, 128))
                parts.append(
                    jnp.where(row16 == k, spread, jnp.where(row16 == k + 8, 1.0, 0.0)).astype(BF16)
                )
            left = jnp.concatenate(parts, axis=1)
            out = jnp.dot(left, wbuf[i], preferred_element_type=F32)
            limit = den[pl.ds(pl.multiple_of(i * 8, 8), 8), :]
            limit = jnp.concatenate([limit, limit], axis=1)
            live = iota((8, 256), 1) < limit
            both.append(
                jnp.concatenate([jnp.where(live, out[0:8], 0.0), jnp.where(live, out[8:16], 0.0)], axis=1)
            )
        whole = jnp.concatenate(both, axis=0)
        high = whole.astype(BF16)
        at = pl.multiple_of(pair * 16, 16)
        contrib[pl.ds(at, 16), :] = high
        contrib[pl.ds(at + 128, 16), :] = (whole - high.astype(F32)).astype(BF16)

    sums = jnp.dot(onehot_t[...], contrib[...], preferred_element_type=F32)
    send_a[...] = sums.reshape(16, 8, 512)

    pl.semaphore_wait(barrier, nx - 1 + jnp.where(s > 0, nx, 0) + jnp.where(s < ns - 1, nx, 0))

    def remote(src, dst, sem_send, sem_recv, ds, dr):
        return pltpu.make_async_remote_copy(
            src_ref=src, dst_ref=dst, send_sem=sem_send, recv_sem=sem_recv,
            device_id=(ds, dr), device_id_type=MESH,
        )

    rounds = (ns - 2).bit_length()

    def steps(k):
        return [(s - (1 << k), s >= 1 << k), (s + (1 << k), s < ns - (1 << k))] if k < rounds else []

    def tell(k):
        for side, (there, ok) in enumerate(steps(k)):

            @pl.when(ok)
            def _():
                pl.semaphore_signal(sem_k.at[2 * k + 1 - side], inc=1, device_id=(there, r), device_id_type=MESH)

    def heard(k):
        for side, (_, ok) in enumerate(steps(k)):

            @pl.when(ok)
            def _():
                pl.semaphore_wait(sem_k.at[2 * k + side], 1)

    @pl.when(s > 0)
    def _():
        for g in range(2):
            remote(send_a.at[g], recv_a.at[nx - 1 + r], sem_s.at[1], sem_a.at[1], s - 1, nx - 2 + g).start()

    @pl.when(s < ns - 1)
    def _():
        for g in range(2):
            remote(send_a.at[10 + g], recv_a.at[nx - 1 + r], sem_s.at[2], sem_a.at[1], s + 1, g).start()

    @pl.loop(1, nx)
    def _(d):
        rp = lax.rem(r + d, nx)
        remote(send_a.at[2 + rp], recv_a.at[d - 1], sem_s.at[0], sem_a.at[0], s, rp).start()

    def sent(ref, sem, cond=None):
        def wait():
            remote(ref, ref, sem, sem_a.at[0], s, r).wait_send()

        pending.append(wait if cond is None else lambda: pl.when(cond)(wait))

    sent(recv_a.at[pl.ds(0, nx - 1)], sem_s.at[0])
    sent(recv_a.at[pl.ds(0, 2)], sem_s.at[1], s > 0)
    sent(recv_a.at[pl.ds(0, 2)], sem_s.at[2], s < ns - 1)
    tell(0)
    ins[3].wait()
    m = meas[...]
    seen = jnp.concatenate(
        [m[v : v + 1, q * 256 : (q + 1) * 256] for v in range(2) for q in range(4)], axis=0
    )
    own = send_a[2 + r]
    remote(send_a.at[pl.ds(0, nx - 1)], recv_a.at[pl.ds(0, nx - 1)], sem_s.at[0], sem_a.at[0], s, r).wait_recv()
    total[...] = own + jnp.sum(recv_a[0 : nx - 1], axis=0)

    @pl.when(jnp.logical_or(low_edge, high_edge))
    def _():
        remote(send_a.at[pl.ds(0, nx)], recv_a.at[pl.ds(nx - 1, nx)], sem_s.at[0], sem_a.at[1], s, r).wait_recv()
        total[...] += jnp.sum(recv_a[nx - 1 : 2 * nx - 1], axis=0)

    tot = total[...]
    corr = (seen - tot[:, 0:256]) / jnp.maximum(tot[:, 256:512], 1.0)
    send_b[...] = corr.astype(BF16)
    recv_b[2 + r] = corr.astype(BF16)

    @pl.when(low_edge)
    def _():
        @pl.loop(0, nx)
        def _(rp):
            remote(send_b, recv_b.at[10 + r], sem_s.at[4], sem_b.at[2], s - 1, rp).start()

    @pl.when(high_edge)
    def _():
        @pl.loop(0, nx)
        def _(rp):
            remote(send_b, recv_b.at[r - (nx - 2)], sem_s.at[4], sem_b.at[1], s + 1, rp).start()

    @pl.loop(1, nx)
    def _(d):
        rp = lax.rem(r + d, nx)
        remote(send_b, recv_b.at[2 + r], sem_s.at[3], sem_b.at[0], s, rp).start()

    heard(0)
    tell(1)
    sent(recv_b.at[pl.ds(0, nx - 1)], sem_s.at[3])
    sent(recv_b.at[pl.ds(0, nx)], sem_s.at[4], jnp.logical_or(low_edge, high_edge))
    for v in range(2):
        for q in range(4):
            cor_ref[v : v + 1, q * 256 : (q + 1) * 256] = corr[v * 4 + q : v * 4 + q + 1, :]

    limit = den[...]
    limit = jnp.concatenate([limit, limit], axis=1)
    live = iota((128, 256), 1) < limit
    live3 = jnp.where(live, 1.0, 0.0).reshape(16, 8, 256)

    remote(recv_b.at[pl.ds(0, nx - 1)], recv_b.at[pl.ds(0, nx - 1)], sem_s.at[3], sem_b.at[0], s, r).wait_recv()

    @pl.when(s > 0)
    def _():
        remote(recv_b.at[pl.ds(0, 2)], recv_b.at[pl.ds(0, 2)], sem_s.at[3], sem_b.at[1], s, r).wait_recv()

    @pl.when(s < ns - 1)
    def _():
        remote(recv_b.at[pl.ds(10, 2)], recv_b.at[pl.ds(10, 2)], sem_s.at[3], sem_b.at[2], s, r).wait_recv()

    heard(1)
    tell(2)
    table = recv_b[...].astype(F32).reshape(128, 256).astype(BF16)
    picked = jnp.dot(onehot[...], table, preferred_element_type=F32)
    picked = jnp.where(live, picked, 0.0).reshape(16, 8, 256)
    lhs_b[...] = jnp.concatenate([picked, live3], axis=1).astype(BF16)

    row8 = iota((8, 128), 0)

    @pl.loop(0, 2)
    def _(p):
        tops, bottoms = [], []
        for x in range(8):
            i = p * 8 + x
            out = lax.dot_general(
                lhs_b[i], wbuf[i], (((1,), (1,)), ((), ())), preferred_element_type=F32
            )
            for rows, into in ((out[0:8], tops), (out[8:16], bottoms)):
                lanes = []
                for t in range(4):
                    k = 2 * t
                    both = jnp.where(row8 == k, rows[:, k * 128 : k * 128 + 128], 0.0) + jnp.where(
                        row8 == k + 1, rows[:, k * 128 + 128 : k * 128 + 256], 0.0
                    )
                    lanes.append(jnp.sum(both, axis=0, keepdims=True))
                into.append(jnp.concatenate(lanes, axis=1))
        num[pl.ds(pl.multiple_of(p * 8, 8), 8), :] = jnp.concatenate(tops, axis=0)
        num[pl.ds(pl.multiple_of(p * 8 + 16, 8), 8), :] = jnp.concatenate(bottoms, axis=0)

    before = vol[...]
    sart = jnp.maximum(before + num[0:groups] / num[groups : 2 * groups], 0.0)
    gap = (sart - before).reshape(2, 8, 512)
    cells3 = sart.reshape(2, 8, 512)

    ublk[...] = cells3

    def exists(ds, dr):
        ok = None
        for cond in (
            [s > 0] if ds < 0 else [s < ns - 1] if ds > 0 else []
        ) + ([r > 0] if dr < 0 else [r < nx - 1] if dr > 0 else []):
            ok = cond if ok is None else jnp.logical_and(ok, cond)
        return ok

    def edge(n, ds, dr):
        if dr == 0:
            src, dst = ublk, uside.at[1 if ds < 0 else 0]
        elif dr < 0:
            src, dst = ublk.at[:, pl.ds(0, 2), :], halo.at[1 - ds, :, pl.ds(0, 2), :]
        else:
            src, dst = ublk.at[:, pl.ds(6, 2), :], halo.at[1 - ds, :, pl.ds(6, 2), :]
        return remote(src, dst, sem_cs.at[n], sem_c.at[n], s + ds, r + dr)

    offsets = [(ds, dr) for ds in (-1, 1) for dr in (-1, 1, 0)] + [(0, -1), (0, 1)]
    for n, (ds, dr) in enumerate(offsets):

        @pl.when(exists(ds, dr))
        def _():
            edge(n, ds, dr).start()

        pending.append(
            lambda n=n, ds=ds, dr=dr: pl.when(exists(ds, dr))(lambda: edge(n, ds, dr).wait_send())
        )

    heard(2)
    tell(3)
    for n, (ds, dr) in enumerate(offsets):

        @pl.when(exists(-ds, -dr))
        def _():
            edge(n, ds, dr).wait_recv()

    heard(3)
    def padded(main, rim):
        return jnp.concatenate([main, rim], axis=1)

    field = jnp.concatenate(
        [padded(uside[0], halo[0]), padded(ublk[...], halo[1]), padded(uside[1], halo[2])], axis=0
    )
    slope = tv_slope(field)

    def reduce_all(n, parts):
        red_s[n] = parts
        others = everyone_else(ns, nx, s, r)
        for j, (ds, dr) in enumerate(others):
            remote(red_s.at[n], red_in.at[n, j], sem_s.at[5 + n], sem_r.at[n], ds, dr).start()
        sent(red_in.at[n], sem_s.at[5 + n])
        remote(red_in.at[n], red_in.at[n], sem_s.at[5 + n], sem_r.at[n], s, r).wait_recv()
        return parts + jnp.sum(red_in[n], axis=0)

    def half(x):
        return x + pltpu.roll(x, 64, 1)

    own_slope = slope[1:3, 0:8, :]
    left = iota((1, 128), 1) < 64
    both = reduce_all(
        0, jnp.where(left, half(lane_partial(gap * gap)), half(lane_partial(own_slope * own_slope)))
    )
    rate = TV_RATE * jnp.sqrt(jnp.sum(jnp.where(left, both, 0.0), axis=1, keepdims=True))
    scale = jnp.sqrt(jnp.sum(jnp.where(left, 0.0, both), axis=1, keepdims=True) + 1e-06)
    inner = field[1:5]
    plane = iota(inner.shape, 0) + jnp.where(s > 0, 1, 0)
    row = iota(inner.shape, 1)
    inside = jnp.logical_and(plane >= 1, iota(inner.shape, 0) < jnp.where(s < ns - 1, 4, 3))
    inside = jnp.logical_and(inside, row < jnp.where(r > 0, 16, 12))
    inside = jnp.logical_and(inside, jnp.logical_or(row < 8, jnp.logical_or(row >= 12, r < nx - 1)))
    step = (rate / scale).reshape(1, 1, 1)
    first_u = jnp.where(inside, inner - step * slope, 0.0)
    slope2 = tv_slope(first_u)[:, 0:8, :]
    both2 = reduce_all(1, lane_partial(slope2 * slope2))
    scale2 = jnp.sqrt(jnp.sum(both2, axis=1, keepdims=True) + 1e-06)
    step2 = (rate / scale2).reshape(1, 1, 1)
    upd_ref[...] = first_u[1:3, 0:8, :] - step2 * slope2

    for wait in pending:
        wait()


def put_out(upd, cor, upd_hbm, cor_hbm, sem):
    copies = [pltpu.make_async_copy(upd, upd_hbm, sem.at[0]), pltpu.make_async_copy(cor, cor_hbm, sem.at[1])]
    for c in copies:
        c.start()
    for c in copies:
        c.wait()


def body(ns, nx, volume, footprint, tile_block, tile_cells, measured):
    any_space = pl.BlockSpec(memory_space=pltpu.HBM)
    vmem = pl.BlockSpec(memory_space=pltpu.VMEM)
    dma = pltpu.SemaphoreType.DMA
    call = pl.pallas_call(
        functools.partial(kernel, ns, nx),
        out_shape=(pltpu.VMEM((2, 8, 512), F32), pltpu.VMEM((2, 1024), F32)),
        in_specs=[any_space] * 5,
        out_specs=(vmem, vmem),
        scratch_shapes=[
            pltpu.VMEM((16, 512), F32),
            pltpu.VMEM((16, 1024, 256), BF16),
            pltpu.VMEM((2, 4, 2, 8), jnp.int32),
            pltpu.VMEM((2, 4, 2, 8), jnp.int32),
            pltpu.VMEM((2, 1024), F32),
            pltpu.VMEM((2, 8, 128), jnp.int32),
            pltpu.VMEM((2, 8, 128), jnp.int32),
            pltpu.VMEM((128, 128), BF16),
            pltpu.VMEM((128, 256), BF16),
            pltpu.VMEM((256, 512), BF16),
            pltpu.VMEM((16, 8, 512), F32),
            pltpu.VMEM((2 * nx - 1, 8, 512), F32),
            pltpu.VMEM((8, 512), F32),
            pltpu.VMEM((8, 256), BF16),
            pltpu.VMEM((16, 8, 256), BF16),
            pltpu.VMEM((16, 16, 256), BF16),
            pltpu.VMEM((32, 512), F32),
            pltpu.VMEM((128, 128), jnp.int32),
            pltpu.VMEM((2, 8, 512), F32),
            pltpu.VMEM((2, 2, 8, 512), F32),
            pltpu.VMEM((3, 2, 8, 512), F32),
            pltpu.VMEM((2, 1, 128), F32),
            pltpu.VMEM((2, ns * nx - 1, 1, 128), F32),
            dma((len(PIECES),)),
            dma((4,)),
            dma((7,)),
            dma((2,)),
            dma((3,)),
            dma((8,)),
            dma((8,)),
            dma((2,)),
            pltpu.SemaphoreType.REGULAR((8,)),
        ],
        compiler_params=pltpu.CompilerParams(
            collective_id=0, has_side_effects=True, vmem_limit_bytes=60 * 1024 * 1024
        ),
    )
    operands = (
        volume.reshape(16, 512),
        footprint.reshape(16, 1024, 256),
        jnp.transpose(tile_block, (0, 2, 3, 1)),
        jnp.transpose(tile_cells, (0, 2, 3, 1)),
        measured,
    )
    results = call(*[pltpu.with_memory_space_constraint(x, pltpu.HBM) for x in operands])
    return pl.pallas_call(
        put_out,
        out_shape=tuple(jax.ShapeDtypeStruct(x.shape, F32) for x in results),
        in_specs=[vmem, vmem],
        out_specs=(any_space, any_space),
        scratch_shapes=[dma((2,))],
        compiler_params=pltpu.CompilerParams(vmem_limit_bytes=1024 * 1024),
    )(*[pltpu.with_memory_space_constraint(x, pltpu.VMEM) for x in results])


def solution(mesh):
    ns, nx = mesh.shape["slab"], mesh.shape["xy"]
    placed = (
        P("slab", "xy", None),
        P("slab", "xy", None, None, None, None),
        P("slab", "xy", None, None),
        P("slab", "xy", None, None),
        P(),
    )
    return jax.shard_map(
        functools.partial(body, ns, nx),
        mesh=mesh,
        in_specs=placed,
        out_specs=(P("slab", "xy", None), P(None, ("slab", "xy"))),
        check_vma=False,
    )
```

```python
import functools

import jax
import jax.numpy as jnp
from jax import lax
from jax.experimental import pallas as pl
from jax.experimental.pallas import tpu as pltpu
from jax.sharding import PartitionSpec as P

TV_RATE = 0.8
SMOOTHING = 0.01
MESH = pl.DeviceIdType.MESH
F32 = jnp.float32
BF16 = jnp.bfloat16
PIECES = ((0, 4), (4, 8), (8, 12), (12, 16))
GROUPS = 12


def iota(shape, dim):
    return lax.broadcasted_iota(jnp.int32, shape, dim)


def lane_next(x):
    return jnp.where(iota(x.shape, 2) < x.shape[2] - 1, pltpu.roll(x, x.shape[2] - 1, 2), 0.0)


def units(field):
    base = field[:-1]
    diff_a = field[1:] - base
    diff_b = pltpu.roll(base, base.shape[1] - 1, 1) - base
    diff_e = lane_next(base) - base
    inv = lax.rsqrt(diff_a * diff_a + diff_b * diff_b + diff_e * diff_e + SMOOTHING)
    return diff_a * inv, diff_b * inv, diff_e * inv


def tv_slope(field):
    unit_a, unit_b, unit_e = units(field)
    core = field[1:-1]
    prev_b = pltpu.roll(unit_b[1:], 1, 1)
    edge = core * lax.rsqrt(core * core + SMOOTHING)
    prev_e = jnp.where(iota(core.shape, 2) == 0, edge, pltpu.roll(unit_e[1:], 1, 2))
    return unit_a[:-1] + prev_b + prev_e - (unit_a + unit_b + unit_e)[1:]


def lane_partial(x):
    rows = jnp.sum(x, axis=0)
    parts = rows[:, :128]
    for c in range(1, x.shape[2] // 128):
        parts = parts + rows[:, c * 128 : (c + 1) * 128]
    return jnp.sum(parts, axis=0, keepdims=True)


def everyone_else(ns, nx, s, r):
    if (ns, nx) != (16, 8):
        return [(lax.rem(s + d // nx, ns), lax.rem(r + d % nx, nx)) for d in range(1, ns * nx)]
    z = ((s // 2) % 2) * 2 + r // 4
    at_x = [((s // 4 + d) % 4) * 4 for d in range(4)]
    at_z = [(z + d) % 4 for d in range(4)]
    at_y = [(r + d) % 4 for d in range(4)]
    at_core = [(s + d) % 2 for d in range(2)]
    slab_z = [(v // 2) * 2 for v in at_z]
    xy_z = [(v % 2) * 4 for v in at_z]
    slab = {
        (dx, dz, dc): at_x[dx] + slab_z[dz] + at_core[dc] for dx in range(4) for dz in range(4) for dc in range(2)
    }
    xy = {(dz, dy): xy_z[dz] + at_y[dy] for dz in range(4) for dy in range(4)}
    moves = [(dx, dz, dy, dc) for dx in range(4) for dz in range(4) for dy in range(4) for dc in range(2)]
    moves.sort(key=lambda m: -sum(min(d, 4 - d) for d in m[:3]) * 2 - m[3])
    return [(slab[dx, dz, dc], xy[dz, dy]) for dx, dz, dy, dc in moves if (dx, dz, dy, dc) != (0, 0, 0, 0)]


def kernel(
    ns, nx,
    vol_hbm, foot_hbm, blk_hbm, cells_hbm, meas_hbm,
    upd_ref, cor_ref,
    vol, wbuf, blk, cells, meas, bcol, ccol, onehot, onehot_t, contrib,
    send_e, send_a, recv_a, total, send_b, recv_b, lhs_b, den,
    ublk, uside, halo,
    red_s, red_in,
    sem_w, sem_in, sem_s, sem_a, sem_b, sem_c, sem_cs, sem_r, sem_k,
):
    s = lax.axis_index("slab")
    r = lax.axis_index("xy")
    groups = wbuf.shape[0]
    low_edge = jnp.logical_and(r < 2, s > 0)
    high_edge = jnp.logical_and(r >= nx - 2, s < ns - 1)
    pending = []
    first = s % 2

    ins = [
        pltpu.make_async_copy(blk_hbm, blk, sem_in.at[0]),
        pltpu.make_async_copy(cells_hbm, cells, sem_in.at[1]),
        pltpu.make_async_copy(vol_hbm.at[first], vol.at[0], sem_in.at[2]),
        pltpu.make_async_copy(vol_hbm.at[1 - first], vol.at[1], sem_in.at[4]),
        pltpu.make_async_copy(
            meas_hbm.at[:, pl.ds(pl.multiple_of((s * nx + r) * 1024, 1024), 1024)], meas, sem_in.at[3]
        ),
    ]
    for c in ins:
        c.start()

    def load(n):
        begin, end = PIECES[n]
        source = lax.rem(begin + first * 8, 16)
        return pltpu.make_async_copy(
            foot_hbm.at[pl.ds(source, end - begin)], wbuf.at[pl.ds(begin, end - begin)], sem_w.at[n]
        )

    for n in range(len(PIECES)):
        load(n).start()

    barrier = pltpu.get_barrier_semaphore()

    def hello(ds, dr):
        pl.semaphore_signal(barrier, inc=1, device_id=(ds, dr), device_id_type=MESH)

    recv_b[...] = jnp.zeros(recv_b.shape, BF16)
    uside[...] = jnp.zeros(uside.shape, F32)
    halo[...] = jnp.zeros(halo.shape, F32)

    @pl.when(s > 0)
    def _():
        for d in range(nx):
            hello(s - 1, d)

    @pl.when(s < ns - 1)
    def _():
        for d in range(nx):
            hello(s + 1, d)

    for d in range(1, nx):
        hello(s, lax.rem(r + d, nx))

    ins[0].wait()
    ins[1].wait()
    for p in range(2):
        for t in range(4):
            bcol[p, 2 * t : 2 * t + 2, 0:8] = blk[p, t]
            ccol[p, 2 * t : 2 * t + 2, 0:8] = cells[p, t]
    lane = iota((8, 128), 1)
    view4 = (iota((8, 128), 0) & 1) * 4
    lowest = (4 * s - 1) * 8
    base = (1 - first) * 16
    hots, near_hots = [], []
    for q in range(2):
        blk_p = bcol[(q + first) % 2]
        cells_p = ccol[(q + first) % 2]
        for x in range(8):
            i = q * 8 + x
            near = jnp.broadcast_to(blk_p[:, x : x + 1], (8, 128)) - lowest
            target = (near >> 2) * 8 + view4 + (near & 3)
            hots.append(jnp.where(lane == target, 1.0, 0.0))
            if q == 1:
                near_hots.append(jnp.where(lane == target - base, 1.0, 0.0))
            den[i * 8 : i * 8 + 8, :] = jnp.broadcast_to(cells_p[:, x : x + 1], (8, 128))
    hot = jnp.concatenate(hots, axis=0)
    onehot[0:64, :] = hot[0:64].astype(BF16)
    onehot[64:128, :] = jnp.concatenate(near_hots, axis=0).astype(BF16)
    hot = jnp.transpose(hot)
    for q in range(2):
        part = hot[:, q * 64 : q * 64 + 64]
        onehot_t[:, q * 128 : q * 128 + 128] = jnp.concatenate([part, part], axis=1).astype(BF16)
    ins[2].wait()
    ins[3].wait()
    row16 = iota((16, 128), 0)

    def forward(slot, pair):
        both = []
        for h in range(2):
            i = pair * 2 + h
            vox = vol[slot, pl.ds(i - slot * 8, 1), :]
            parts = []
            for k in range(8):
                t = k // 2
                spread = jnp.broadcast_to(vox[:, t * 128 : (t + 1) * 128], (16, 128))
                parts.append(
                    jnp.where(row16 == k, spread, jnp.where(row16 == k + 8, 1.0, 0.0)).astype(BF16)
                )
            left = jnp.concatenate(parts, axis=1)
            out = jnp.dot(left, wbuf[i], preferred_element_type=F32)
            limit = den[pl.ds(pl.multiple_of(i * 8, 8), 8), :]
            limit = jnp.concatenate([limit, limit], axis=1)
            live = iota((8, 256), 1) < limit
            both.append(
                jnp.concatenate([jnp.where(live, out[0:8], 0.0), jnp.where(live, out[8:16], 0.0)], axis=1)
            )
        whole = jnp.concatenate(both, axis=0)
        high = whole.astype(BF16)
        at = pl.multiple_of(pair * 16 + slot * 64, 16)
        contrib[pl.ds(at, 16), :] = high
        contrib[pl.ds(at + 64, 16), :] = (whole - high.astype(F32)).astype(BF16)

    def forward_slot(slot):
        @pl.loop(slot * 4, slot * 4 + 4)
        def _(pair):
            for n, (begin, _) in enumerate(PIECES):
                if begin // 8 == slot:

                    @pl.when(pair * 2 == begin)
                    def _(n=n):
                        load(n).wait()

            forward(slot, pair)

        k = slice(slot * 128, slot * 128 + 128)
        sums = jnp.dot(onehot_t[:, k], contrib[k, :], preferred_element_type=F32)
        return sums.reshape(16, 8, 512)

    send_e[...] = forward_slot(0)

    pl.semaphore_wait(barrier, nx - 1 + jnp.where(s > 0, nx, 0) + jnp.where(s < ns - 1, nx, 0))

    def remote(src, dst, sem_send, sem_recv, ds, dr):
        return pltpu.make_async_remote_copy(
            src_ref=src, dst_ref=dst, send_sem=sem_send, recv_sem=sem_recv,
            device_id=(ds, dr), device_id_type=MESH,
        )

    rounds = (ns - 2).bit_length()

    def steps(k):
        return [(s - (1 << k), s >= 1 << k), (s + (1 << k), s < ns - (1 << k))] if k < rounds else []

    def tell(k):
        for side, (there, ok) in enumerate(steps(k)):

            @pl.when(ok)
            def _():
                pl.semaphore_signal(sem_k.at[2 * k + 1 - side], inc=1, device_id=(there, r), device_id_type=MESH)

    def heard(k):
        for side, (_, ok) in enumerate(steps(k)):

            @pl.when(ok)
            def _():
                pl.semaphore_wait(sem_k.at[2 * k + side], 1)

    @pl.when(jnp.logical_and(first == 0, s > 0))
    def _():
        for g in range(2):
            remote(send_e.at[g], recv_a.at[nx - 1 + r], sem_s.at[1], sem_a.at[1], s - 1, nx - 2 + g).start()

    @pl.when(jnp.logical_and(first == 1, s < ns - 1))
    def _():
        for g in range(2):
            remote(send_e.at[10 + g], recv_a.at[nx - 1 + r], sem_s.at[2], sem_a.at[1], s + 1, g).start()

    send_a[...] = send_e[...] + forward_slot(1)

    @pl.loop(1, nx)
    def _(d):
        rp = lax.rem(r + d, nx)
        remote(send_a.at[2 + rp], recv_a.at[d - 1], sem_s.at[0], sem_a.at[0], s, rp).start()

    @pl.when(jnp.logical_and(first == 1, s > 0))
    def _():
        for g in range(2):
            remote(send_a.at[g], recv_a.at[nx - 1 + r], sem_s.at[1], sem_a.at[1], s - 1, nx - 2 + g).start()

    @pl.when(jnp.logical_and(first == 0, s < ns - 1))
    def _():
        for g in range(2):
            remote(send_a.at[10 + g], recv_a.at[nx - 1 + r], sem_s.at[2], sem_a.at[1], s + 1, g).start()

    def sent(ref, sem, cond=None):
        def wait():
            remote(ref, ref, sem, sem_a.at[0], s, r).wait_send()

        pending.append(wait if cond is None else lambda: pl.when(cond)(wait))

    sent(recv_a.at[pl.ds(0, nx - 1)], sem_s.at[0])
    sent(recv_a.at[pl.ds(0, 2)], sem_s.at[1], s > 0)
    sent(recv_a.at[pl.ds(0, 2)], sem_s.at[2], s < ns - 1)
    tell(0)
    ins[4].wait()
    m = meas[...]
    seen = jnp.concatenate(
        [m[v : v + 1, q * 256 : (q + 1) * 256] for v in range(2) for q in range(4)], axis=0
    )
    own = send_a[2 + r]
    remote(send_a.at[pl.ds(0, nx - 1)], recv_a.at[pl.ds(0, nx - 1)], sem_s.at[0], sem_a.at[0], s, r).wait_recv()
    total[...] = own + jnp.sum(recv_a[0 : nx - 1], axis=0)

    @pl.when(jnp.logical_or(low_edge, high_edge))
    def _():
        remote(send_a.at[pl.ds(0, nx)], recv_a.at[pl.ds(nx - 1, nx)], sem_s.at[0], sem_a.at[1], s, r).wait_recv()
        total[...] += jnp.sum(recv_a[nx - 1 : 2 * nx - 1], axis=0)

    tot = total[...]
    corr = (seen - tot[:, 0:256]) / jnp.maximum(tot[:, 256:512], 1.0)
    send_b[...] = corr.astype(BF16)
    recv_b[2 + r] = corr.astype(BF16)

    @pl.when(low_edge)
    def _():
        @pl.loop(0, nx)
        def _(rp):
            remote(send_b, recv_b.at[10 + r], sem_s.at[4], sem_b.at[2], s - 1, rp).start()

    @pl.when(high_edge)
    def _():
        @pl.loop(0, nx)
        def _(rp):
            remote(send_b, recv_b.at[r - (nx - 2)], sem_s.at[4], sem_b.at[1], s + 1, rp).start()

    @pl.loop(1, nx)
    def _(d):
        rp = lax.rem(r + d, nx)
        remote(send_b, recv_b.at[2 + r], sem_s.at[3], sem_b.at[0], s, rp).start()

    heard(0)
    tell(1)
    sent(recv_b.at[pl.ds(0, nx - 1)], sem_s.at[3])
    sent(recv_b.at[pl.ds(0, nx)], sem_s.at[4], jnp.logical_or(low_edge, high_edge))
    for v in range(2):
        for q in range(4):
            cor_ref[v : v + 1, q * 256 : (q + 1) * 256] = corr[v * 4 + q : v * 4 + q + 1, :]

    limit = den[...]
    limit = jnp.concatenate([limit, limit], axis=1)
    live = iota((128, 256), 1) < limit
    live3 = jnp.where(live, 1.0, 0.0).reshape(16, 8, 256)

    def arrived(sem, cond):
        @pl.when(cond)
        def _():
            remote(recv_b.at[pl.ds(0, 2)], recv_b.at[pl.ds(0, 2)], sem_s.at[3], sem, s, r).wait_recv()

    row8 = iota((8, 128), 0)

    def back(slot, table):
        half = slice(slot * 64, slot * 64 + 64)
        table = table.astype(F32).reshape(table.shape[0] * 8, 256).astype(BF16)
        hot = onehot[half, :]
        found = jnp.dot(hot, table, preferred_element_type=F32)
        found = jnp.where(live[half], found, 0.0).reshape(8, 8, 256)
        lhs_b[slot * 8 : slot * 8 + 8] = jnp.concatenate([found, live3[slot * 8 : slot * 8 + 8]], axis=1).astype(BF16)
        tops, bottoms = [], []
        for x in range(8):
            i = slot * 8 + x
            out = lax.dot_general(
                lhs_b[i], wbuf[i], (((1,), (1,)), ((), ())), preferred_element_type=F32
            )
            for rows, into in ((out[0:8], tops), (out[8:16], bottoms)):
                lanes = []
                for t in range(4):
                    k = 2 * t
                    both = jnp.where(row8 == k, rows[:, k * 128 : k * 128 + 128], 0.0) + jnp.where(
                        row8 == k + 1, rows[:, k * 128 + 128 : k * 128 + 256], 0.0
                    )
                    lanes.append(jnp.sum(both, axis=0, keepdims=True))
                into.append(jnp.concatenate(lanes, axis=1))
        shift = jnp.concatenate(tops, axis=0) / jnp.concatenate(bottoms, axis=0)
        sart = jnp.maximum(vol[slot] + shift, 0.0)
        ublk[(slot + first) % 2] = sart
        return sart - vol[slot]

    remote(recv_b.at[pl.ds(0, nx - 1)], recv_b.at[pl.ds(0, nx - 1)], sem_s.at[3], sem_b.at[0], s, r).wait_recv()
    arrived(sem_b.at[1], jnp.logical_and(first == 1, s > 0))
    arrived(sem_b.at[2], jnp.logical_and(first == 0, s < ns - 1))
    heard(1)
    tell(2)
    pad = jnp.zeros((6, 8, 256), BF16)
    gap1 = back(1, jnp.concatenate([recv_b[pl.ds((1 - first) * 2, 10)], pad], axis=0))
    arrived(sem_b.at[1], jnp.logical_and(first == 0, s > 0))
    arrived(sem_b.at[2], jnp.logical_and(first == 1, s < ns - 1))
    gap0 = back(0, recv_b[...])
    gap = jnp.concatenate([gap0[None], gap1[None]], axis=0)


    def exists(ds, dr):
        ok = None
        for cond in (
            [s > 0] if ds < 0 else [s < ns - 1] if ds > 0 else []
        ) + ([r > 0] if dr < 0 else [r < nx - 1] if dr > 0 else []):
            ok = cond if ok is None else jnp.logical_and(ok, cond)
        return ok

    def edge(n, ds, dr):
        if dr == 0:
            src, dst = ublk, uside.at[1 if ds < 0 else 0]
        elif dr < 0:
            src, dst = ublk.at[:, pl.ds(0, 2), :], halo.at[1 - ds, :, pl.ds(0, 2), :]
        else:
            src, dst = ublk.at[:, pl.ds(6, 2), :], halo.at[1 - ds, :, pl.ds(6, 2), :]
        return remote(src, dst, sem_cs.at[n], sem_c.at[n], s + ds, r + dr)

    offsets = [(ds, dr) for ds in (-1, 1) for dr in (-1, 1, 0)] + [(0, -1), (0, 1)]
    for n, (ds, dr) in enumerate(offsets):

        @pl.when(exists(ds, dr))
        def _():
            edge(n, ds, dr).start()

        pending.append(
            lambda n=n, ds=ds, dr=dr: pl.when(exists(ds, dr))(lambda: edge(n, ds, dr).wait_send())
        )

    heard(2)
    tell(3)
    for n, (ds, dr) in enumerate(offsets):

        @pl.when(exists(-ds, -dr))
        def _():
            edge(n, ds, dr).wait_recv()

    heard(3)
    def padded(main, rim):
        return jnp.concatenate([main, rim], axis=1)

    field = jnp.concatenate(
        [padded(uside[0], halo[0]), padded(ublk[...], halo[1]), padded(uside[1], halo[2])], axis=0
    )
    slope = tv_slope(field)

    def reduce_all(n, parts):
        red_s[n] = parts
        others = everyone_else(ns, nx, s, r)
        for j, (ds, dr) in enumerate(others):
            remote(red_s.at[n], red_in.at[n, j], sem_s.at[5 + n], sem_r.at[n], ds, dr).start()
        sent(red_in.at[n], sem_s.at[5 + n])
        remote(red_in.at[n], red_in.at[n], sem_s.at[5 + n], sem_r.at[n], s, r).wait_recv()
        return parts + jnp.sum(red_in[n], axis=0)

    def half(x):
        return x + pltpu.roll(x, 64, 1)

    own_slope = slope[1:3, 0:8, :]
    left = iota((1, 128), 1) < 64
    both = reduce_all(
        0, jnp.where(left, half(lane_partial(gap * gap)), half(lane_partial(own_slope * own_slope)))
    )
    rate = TV_RATE * jnp.sqrt(jnp.sum(jnp.where(left, both, 0.0), axis=1, keepdims=True))
    scale = jnp.sqrt(jnp.sum(jnp.where(left, 0.0, both), axis=1, keepdims=True) + 1e-06)
    inner = field[1:5]
    plane = iota(inner.shape, 0) + jnp.where(s > 0, 1, 0)
    row = iota(inner.shape, 1)
    inside = jnp.logical_and(plane >= 1, iota(inner.shape, 0) < jnp.where(s < ns - 1, 4, 3))
    inside = jnp.logical_and(inside, row < jnp.where(r > 0, 16, 12))
    inside = jnp.logical_and(inside, jnp.logical_or(row < 8, jnp.logical_or(row >= 12, r < nx - 1)))
    step = (rate / scale).reshape(1, 1, 1)
    first_u = jnp.where(inside, inner - step * slope, 0.0)
    slope2 = tv_slope(first_u)[:, 0:8, :]
    both2 = reduce_all(1, lane_partial(slope2 * slope2))
    scale2 = jnp.sqrt(jnp.sum(both2, axis=1, keepdims=True) + 1e-06)
    step2 = (rate / scale2).reshape(1, 1, 1)
    upd_ref[...] = first_u[1:3, 0:8, :] - step2 * slope2

    for wait in pending:
        wait()


def put_out(upd, cor, upd_hbm, cor_hbm, sem):
    copies = [pltpu.make_async_copy(upd, upd_hbm, sem.at[0]), pltpu.make_async_copy(cor, cor_hbm, sem.at[1])]
    for c in copies:
        c.start()
    for c in copies:
        c.wait()


def body(ns, nx, volume, footprint, tile_block, tile_cells, measured):
    any_space = pl.BlockSpec(memory_space=pltpu.HBM)
    vmem = pl.BlockSpec(memory_space=pltpu.VMEM)
    dma = pltpu.SemaphoreType.DMA
    call = pl.pallas_call(
        functools.partial(kernel, ns, nx),
        out_shape=(pltpu.VMEM((2, 8, 512), F32), pltpu.VMEM((2, 1024), F32)),
        in_specs=[any_space] * 5,
        out_specs=(vmem, vmem),
        scratch_shapes=[
            pltpu.VMEM((2, 8, 512), F32),
            pltpu.VMEM((16, 1024, 256), BF16),
            pltpu.VMEM((2, 4, 2, 8), jnp.int32),
            pltpu.VMEM((2, 4, 2, 8), jnp.int32),
            pltpu.VMEM((2, 1024), F32),
            pltpu.VMEM((2, 8, 128), jnp.int32),
            pltpu.VMEM((2, 8, 128), jnp.int32),
            pltpu.VMEM((128, 128), BF16),
            pltpu.VMEM((128, 256), BF16),
            pltpu.VMEM((256, 512), BF16),
            pltpu.VMEM((16, 8, 512), F32),
            pltpu.VMEM((16, 8, 512), F32),
            pltpu.VMEM((2 * nx - 1, 8, 512), F32),
            pltpu.VMEM((8, 512), F32),
            pltpu.VMEM((8, 256), BF16),
            pltpu.VMEM((16, 8, 256), BF16),
            pltpu.VMEM((16, 16, 256), BF16),
            pltpu.VMEM((128, 128), jnp.int32),
            pltpu.VMEM((2, 8, 512), F32),
            pltpu.VMEM((2, 2, 8, 512), F32),
            pltpu.VMEM((3, 2, 8, 512), F32),
            pltpu.VMEM((2, 1, 128), F32),
            pltpu.VMEM((2, ns * nx - 1, 1, 128), F32),
            dma((len(PIECES),)),
            dma((5,)),
            dma((7,)),
            dma((2,)),
            dma((3,)),
            dma((8,)),
            dma((8,)),
            dma((2,)),
            pltpu.SemaphoreType.REGULAR((8,)),
        ],
        compiler_params=pltpu.CompilerParams(
            collective_id=0, has_side_effects=True, vmem_limit_bytes=60 * 1024 * 1024
        ),
    )
    operands = (
        volume,
        footprint.reshape(16, 1024, 256),
        jnp.transpose(tile_block, (0, 2, 3, 1)),
        jnp.transpose(tile_cells, (0, 2, 3, 1)),
        measured,
    )
    results = call(*[pltpu.with_memory_space_constraint(x, pltpu.HBM) for x in operands])
    return pl.pallas_call(
        put_out,
        out_shape=tuple(jax.ShapeDtypeStruct(x.shape, F32) for x in results),
        in_specs=[vmem, vmem],
        out_specs=(any_space, any_space),
        scratch_shapes=[dma((2,))],
        compiler_params=pltpu.CompilerParams(vmem_limit_bytes=1024 * 1024),
    )(*[pltpu.with_memory_space_constraint(x, pltpu.VMEM) for x in results])


def solution(mesh):
    ns, nx = mesh.shape["slab"], mesh.shape["xy"]
    placed = (
        P("slab", "xy", None),
        P("slab", "xy", None, None, None, None),
        P("slab", "xy", None, None),
        P("slab", "xy", None, None),
        P(),
    )
    return jax.shard_map(
        functools.partial(body, ns, nx),
        mesh=mesh,
        in_specs=placed,
        out_specs=(P("slab", "xy", None), P(None, ("slab", "xy"))),
        check_vma=False,
    )
```

```python
import functools

import jax
import jax.numpy as jnp
from jax import lax
from jax.experimental import pallas as pl
from jax.experimental.pallas import tpu as pltpu
from jax.sharding import PartitionSpec as P

TV_RATE = 0.8
SMOOTHING = 0.01
MESH = pl.DeviceIdType.MESH
F32 = jnp.float32
BF16 = jnp.bfloat16
PIECES = ((0, 4), (4, 8), (8, 12), (12, 16))
GROUPS = 12


def iota(shape, dim):
    return lax.broadcasted_iota(jnp.int32, shape, dim)


def lane_next(x):
    return jnp.where(iota(x.shape, 2) < x.shape[2] - 1, pltpu.roll(x, x.shape[2] - 1, 2), 0.0)


def units(field):
    base = field[:-1]
    diff_a = field[1:] - base
    diff_b = pltpu.roll(base, base.shape[1] - 1, 1) - base
    diff_e = lane_next(base) - base
    inv = lax.rsqrt(diff_a * diff_a + diff_b * diff_b + diff_e * diff_e + SMOOTHING)
    return diff_a * inv, diff_b * inv, diff_e * inv


def tv_slope(field):
    unit_a, unit_b, unit_e = units(field)
    core = field[1:-1]
    prev_b = pltpu.roll(unit_b[1:], 1, 1)
    edge = core * lax.rsqrt(core * core + SMOOTHING)
    prev_e = jnp.where(iota(core.shape, 2) == 0, edge, pltpu.roll(unit_e[1:], 1, 2))
    return unit_a[:-1] + prev_b + prev_e - (unit_a + unit_b + unit_e)[1:]


def lane_partial(x):
    rows = jnp.sum(x, axis=0)
    parts = rows[:, :128]
    for c in range(1, x.shape[2] // 128):
        parts = parts + rows[:, c * 128 : (c + 1) * 128]
    return jnp.sum(parts, axis=0, keepdims=True)


def everyone_else(ns, nx, s, r):
    if (ns, nx) != (16, 8):
        return [(lax.rem(s + d // nx, ns), lax.rem(r + d % nx, nx)) for d in range(1, ns * nx)]
    z = ((s // 2) % 2) * 2 + r // 4
    at_x = [((s // 4 + d) % 4) * 4 for d in range(4)]
    at_z = [(z + d) % 4 for d in range(4)]
    at_y = [(r + d) % 4 for d in range(4)]
    at_core = [(s + d) % 2 for d in range(2)]
    slab_z = [(v // 2) * 2 for v in at_z]
    xy_z = [(v % 2) * 4 for v in at_z]
    slab = {
        (dx, dz, dc): at_x[dx] + slab_z[dz] + at_core[dc] for dx in range(4) for dz in range(4) for dc in range(2)
    }
    xy = {(dz, dy): xy_z[dz] + at_y[dy] for dz in range(4) for dy in range(4)}
    moves = [(dx, dz, dy, dc) for dx in range(4) for dz in range(4) for dy in range(4) for dc in range(2)]
    moves.sort(key=lambda m: -sum(min(d, 4 - d) for d in m[:3]) * 2 - m[3])
    return [(slab[dx, dz, dc], xy[dz, dy]) for dx, dz, dy, dc in moves if (dx, dz, dy, dc) != (0, 0, 0, 0)]


def kernel(
    ns, nx,
    vol_hbm, foot_hbm, blk_hbm, cells_hbm, meas_hbm,
    upd_ref, cor_ref,
    vol, wbuf, blk, cells, meas, bcol, ccol, onehot, onehot_t, contrib,
    send_e, send_a, recv_a, total, send_b, recv_b, lhs_b, den,
    ublk, uside, halo,
    red_s, red_in,
    sem_w, sem_in, sem_s, sem_a, sem_b, sem_c, sem_cs, sem_r, sem_k,
):
    s = lax.axis_index("slab")
    r = lax.axis_index("xy")
    groups = wbuf.shape[0]
    low_edge = jnp.logical_and(r < 2, s > 0)
    high_edge = jnp.logical_and(r >= nx - 2, s < ns - 1)
    pending = []
    first = s % 2
    slow_owner = jnp.logical_or(jnp.logical_and(first == 0, r < 2), jnp.logical_and(first == 1, r >= nx - 2))

    ins = [
        pltpu.make_async_copy(blk_hbm, blk, sem_in.at[0]),
        pltpu.make_async_copy(cells_hbm, cells, sem_in.at[1]),
        pltpu.make_async_copy(vol_hbm.at[first], vol.at[0], sem_in.at[2]),
        pltpu.make_async_copy(vol_hbm.at[1 - first], vol.at[1], sem_in.at[4]),
        pltpu.make_async_copy(
            meas_hbm.at[:, pl.ds(pl.multiple_of((s * nx + r) * 1024, 1024), 1024)], meas, sem_in.at[3]
        ),
    ]
    for c in ins:
        c.start()

    def load(n):
        begin, end = PIECES[n]
        source = lax.rem(begin + first * 8, 16)
        return pltpu.make_async_copy(
            foot_hbm.at[pl.ds(source, end - begin)], wbuf.at[pl.ds(begin, end - begin)], sem_w.at[n]
        )

    for n in range(len(PIECES)):
        load(n).start()

    barrier = pltpu.get_barrier_semaphore()

    def hello(ds, dr):
        pl.semaphore_signal(barrier, inc=1, device_id=(ds, dr), device_id_type=MESH)

    recv_b[...] = jnp.zeros(recv_b.shape, BF16)
    uside[...] = jnp.zeros(uside.shape, F32)
    recv_a[0 : nx - 1] = jnp.zeros((nx - 1, 8, 512), F32)
    halo[...] = jnp.zeros(halo.shape, F32)

    @pl.when(s > 0)
    def _():
        for d in range(nx):
            hello(s - 1, d)

    @pl.when(s < ns - 1)
    def _():
        for d in range(nx):
            hello(s + 1, d)

    for d in range(1, nx):
        hello(s, lax.rem(r + d, nx))

    ins[0].wait()
    ins[1].wait()
    for p in range(2):
        for t in range(4):
            bcol[p, 2 * t : 2 * t + 2, 0:8] = blk[p, t]
            ccol[p, 2 * t : 2 * t + 2, 0:8] = cells[p, t]
    lane = iota((8, 128), 1)
    view4 = (iota((8, 128), 0) & 1) * 4
    lowest = (4 * s - 1) * 8
    base = (1 - first) * 32
    hots, near_hots = [], []
    for q in range(2):
        blk_p = bcol[(q + first) % 2]
        cells_p = ccol[(q + first) % 2]
        for x in range(8):
            i = q * 8 + x
            near = jnp.broadcast_to(blk_p[:, x : x + 1], (8, 128)) - lowest
            target = (near >> 2) * 8 + view4 + (near & 3)
            hots.append(jnp.where(lane == target, 1.0, 0.0))
            if q == 1:
                near_hots.append(jnp.where(lane == target - base, 1.0, 0.0))
            den[i * 8 : i * 8 + 8, :] = jnp.broadcast_to(cells_p[:, x : x + 1], (8, 128))
    hot = jnp.concatenate(hots, axis=0)
    onehot[0:64, :] = hot[0:64].astype(BF16)
    onehot[64:128, :] = jnp.concatenate(near_hots, axis=0).astype(BF16)
    hot = jnp.transpose(hot)
    for q in range(2):
        part = hot[:, q * 64 : q * 64 + 64]
        onehot_t[:, q * 128 : q * 128 + 128] = jnp.concatenate([part, part], axis=1).astype(BF16)
    ins[2].wait()
    ins[3].wait()
    row16 = iota((16, 128), 0)

    def forward(slot, pair):
        both = []
        for h in range(2):
            i = pair * 2 + h
            vox = vol[slot, pl.ds(i - slot * 8, 1), :]
            parts = []
            for k in range(8):
                t = k // 2
                spread = jnp.broadcast_to(vox[:, t * 128 : (t + 1) * 128], (16, 128))
                parts.append(
                    jnp.where(row16 == k, spread, jnp.where(row16 == k + 8, 1.0, 0.0)).astype(BF16)
                )
            left = jnp.concatenate(parts, axis=1)
            out = jnp.dot(left, wbuf[i], preferred_element_type=F32)
            limit = den[pl.ds(pl.multiple_of(i * 8, 8), 8), :]
            limit = jnp.concatenate([limit, limit], axis=1)
            live = iota((8, 256), 1) < limit
            both.append(
                jnp.concatenate([jnp.where(live, out[0:8], 0.0), jnp.where(live, out[8:16], 0.0)], axis=1)
            )
        whole = jnp.concatenate(both, axis=0)
        high = whole.astype(BF16)
        at = pl.multiple_of(pair * 16 + slot * 64, 16)
        contrib[pl.ds(at, 16), :] = high
        contrib[pl.ds(at + 64, 16), :] = (whole - high.astype(F32)).astype(BF16)

    def forward_slot(slot):
        @pl.loop(slot * 4, slot * 4 + 4)
        def _(pair):
            for n, (begin, _) in enumerate(PIECES):
                if begin // 8 == slot:

                    @pl.when(pair * 2 == begin)
                    def _(n=n):
                        load(n).wait()

            forward(slot, pair)

        k = slice(slot * 128, slot * 128 + 128)
        sums = jnp.dot(onehot_t[:, k], contrib[k, :], preferred_element_type=F32)
        return sums.reshape(16, 8, 512)

    send_e[...] = forward_slot(0)

    pl.semaphore_wait(barrier, nx - 1 + jnp.where(s > 0, nx, 0) + jnp.where(s < ns - 1, nx, 0))

    def remote(src, dst, sem_send, sem_recv, ds, dr):
        return pltpu.make_async_remote_copy(
            src_ref=src, dst_ref=dst, send_sem=sem_send, recv_sem=sem_recv,
            device_id=(ds, dr), device_id_type=MESH,
        )

    rounds = (ns - 2).bit_length()

    def steps(k):
        return [(s - (1 << k), s >= 1 << k), (s + (1 << k), s < ns - (1 << k))] if k < rounds else []

    def tell(k):
        for side, (there, ok) in enumerate(steps(k)):

            @pl.when(ok)
            def _():
                pl.semaphore_signal(sem_k.at[2 * k + 1 - side], inc=1, device_id=(there, r), device_id_type=MESH)

    def heard(k):
        for side, (_, ok) in enumerate(steps(k)):

            @pl.when(ok)
            def _():
                pl.semaphore_wait(sem_k.at[2 * k + side], 1)

    @pl.when(jnp.logical_and(first == 0, s > 0))
    def _():
        for g in range(2):
            remote(send_e.at[g], recv_a.at[nx - 1 + r], sem_s.at[1], sem_a.at[1], s - 1, nx - 2 + g).start()

    @pl.when(jnp.logical_and(first == 1, s < ns - 1))
    def _():
        for g in range(2):
            remote(send_e.at[10 + g], recv_a.at[nx - 1 + r], sem_s.at[2], sem_a.at[1], s + 1, g).start()

    send_a[...] = send_e[...] + forward_slot(1)

    @pl.loop(1, nx)
    def _(d):
        rp = lax.rem(r + d, nx)
        for v, ok in ((0, True), (1, jnp.where(rp % 2 == 0, r <= 4, r >= 3))):
            at = pl.ds(4 * v, 4)

            @pl.when(ok)
            def _(v=v, at=at):
                remote(
                    send_a.at[2 + rp, at], recv_a.at[d - 1, at], sem_s.at[7 * v], sem_a.at[2 * v], s, rp
                ).start()

    @pl.when(jnp.logical_and(first == 1, s > 0))
    def _():
        for g in range(2):
            remote(send_a.at[g], recv_a.at[nx - 1 + r], sem_s.at[1], sem_a.at[1], s - 1, nx - 2 + g).start()

    @pl.when(jnp.logical_and(first == 0, s < ns - 1))
    def _():
        for g in range(2):
            remote(send_a.at[10 + g], recv_a.at[nx - 1 + r], sem_s.at[2], sem_a.at[1], s + 1, g).start()

    def sent(ref, sem, cond=None):
        def wait():
            remote(ref, ref, sem, sem_a.at[0], s, r).wait_send()

        pending.append(wait if cond is None else lambda: pl.when(cond)(wait))

    sent(recv_a.at[pl.ds(0, nx - 1), pl.ds(0, 4)], sem_s.at[0])
    middle = jnp.logical_or(r == 3, r == 4)
    self_half = jnp.where(r % 2 == 0, r <= 4, r >= 3)
    sent(recv_a.at[pl.ds(0, nx - 1), pl.ds(0, 4)], sem_s.at[7], middle)
    outer = jnp.logical_not(middle)
    sent(recv_a.at[pl.ds(0, 3), pl.ds(0, 4)], sem_s.at[7], jnp.logical_and(outer, self_half))
    sent(recv_a.at[pl.ds(0, 4), pl.ds(0, 4)], sem_s.at[7], jnp.logical_and(outer, jnp.logical_not(self_half)))
    sent(recv_a.at[pl.ds(0, 2)], sem_s.at[1], s > 0)
    sent(recv_a.at[pl.ds(0, 2)], sem_s.at[2], s < ns - 1)
    tell(0)
    ins[4].wait()
    m = meas[...]
    seen = jnp.concatenate(
        [m[v : v + 1, q * 256 : (q + 1) * 256] for v in range(2) for q in range(4)], axis=0
    )
    own = send_a[2 + r]
    part = recv_a.at[pl.ds(0, nx - 1), pl.ds(0, 4)]
    remote(part, part, sem_s.at[0], sem_a.at[0], s, r).wait_recv()
    for n, ok in ((4, self_half), (5, jnp.logical_not(self_half))):

        @pl.when(ok)
        def _(n=n):
            part = recv_a.at[pl.ds(0, n), pl.ds(0, 4)]
            remote(part, part, sem_s.at[0], sem_a.at[2], s, r).wait_recv()

    total[...] = own + jnp.sum(recv_a[0 : nx - 1], axis=0)

    @pl.when(jnp.logical_or(low_edge, high_edge))
    def _():
        remote(send_a.at[pl.ds(0, nx)], recv_a.at[pl.ds(nx - 1, nx)], sem_s.at[0], sem_a.at[1], s, r).wait_recv()
        total[...] += jnp.sum(recv_a[nx - 1 : 2 * nx - 1], axis=0)

    tot = total[...]
    corr = (seen - tot[:, 0:256]) / jnp.maximum(tot[:, 256:512], 1.0)
    send_b[...] = corr.astype(BF16)
    recv_b[2 + r] = corr.astype(BF16)

    @pl.when(low_edge)
    def _():
        @pl.loop(0, nx)
        def _(rp):
            remote(send_b, recv_b.at[10 + r], sem_s.at[4], sem_b.at[2], s - 1, rp).start()

    @pl.when(high_edge)
    def _():
        @pl.loop(0, nx)
        def _(rp):
            remote(send_b, recv_b.at[r - (nx - 2)], sem_s.at[4], sem_b.at[1], s + 1, rp).start()

    @pl.loop(1, nx)
    def _(d):
        rp = lax.rem(r + d, nx)
        remote(send_b, recv_b.at[2 + r], sem_s.at[3], sem_b.at[jnp.where(slow_owner, 3, 0)], s, rp).start()

    heard(0)
    tell(1)
    sent(recv_b.at[pl.ds(0, nx - 1)], sem_s.at[3])
    sent(recv_b.at[pl.ds(0, nx)], sem_s.at[4], jnp.logical_or(low_edge, high_edge))
    for v in range(2):
        for q in range(4):
            cor_ref[v : v + 1, q * 256 : (q + 1) * 256] = corr[v * 4 + q : v * 4 + q + 1, :]

    limit = den[...]
    limit = jnp.concatenate([limit, limit], axis=1)
    live = iota((128, 256), 1) < limit
    live3 = jnp.where(live, 1.0, 0.0).reshape(16, 8, 256)

    def arrived(sem, cond, n=2):
        @pl.when(cond)
        def _():
            remote(recv_b.at[pl.ds(0, n)], recv_b.at[pl.ds(0, n)], sem_s.at[3], sem, s, r).wait_recv()

    other_owner = jnp.logical_not(slow_owner)
    row8 = iota((8, 128), 0)

    def back(slot, table):
        half = slice(slot * 64, slot * 64 + 64)
        table = table.astype(F32).reshape(table.shape[0] * 8, 256).astype(BF16)
        hot = onehot[half, :]
        found = jnp.dot(hot, table, preferred_element_type=F32)
        found = jnp.where(live[half], found, 0.0).reshape(8, 8, 256)
        lhs_b[slot * 8 : slot * 8 + 8] = jnp.concatenate([found, live3[slot * 8 : slot * 8 + 8]], axis=1).astype(BF16)
        tops, bottoms = [], []
        for x in range(8):
            i = slot * 8 + x
            out = lax.dot_general(
                lhs_b[i], wbuf[i], (((1,), (1,)), ((), ())), preferred_element_type=F32
            )
            for rows, into in ((out[0:8], tops), (out[8:16], bottoms)):
                lanes = []
                for t in range(4):
                    k = 2 * t
                    both = jnp.where(row8 == k, rows[:, k * 128 : k * 128 + 128], 0.0) + jnp.where(
                        row8 == k + 1, rows[:, k * 128 + 128 : k * 128 + 256], 0.0
                    )
                    lanes.append(jnp.sum(both, axis=0, keepdims=True))
                into.append(jnp.concatenate(lanes, axis=1))
        shift = jnp.concatenate(tops, axis=0) / jnp.concatenate(bottoms, axis=0)
        sart = jnp.maximum(vol[slot] + shift, 0.0)
        ublk[(slot + first) % 2] = sart
        return sart - vol[slot]

    arrived(sem_b.at[0], slow_owner, nx - 2)
    arrived(sem_b.at[0], other_owner, nx - 3)
    arrived(sem_b.at[1], jnp.logical_and(first == 1, s > 0))
    arrived(sem_b.at[2], jnp.logical_and(first == 0, s < ns - 1))
    heard(1)
    tell(2)
    pad = jnp.zeros((8, 8, 256), BF16)
    gap1 = back(1, jnp.concatenate([recv_b[pl.ds((1 - first) * 4, 8)], pad], axis=0))
    arrived(sem_b.at[1], jnp.logical_and(first == 0, s > 0))
    arrived(sem_b.at[2], jnp.logical_and(first == 1, s < ns - 1))
    arrived(sem_b.at[3], slow_owner, 1)
    arrived(sem_b.at[3], other_owner)
    gap0 = back(0, recv_b[...])
    gap = jnp.concatenate([gap0[None], gap1[None]], axis=0)


    def exists(ds, dr):
        ok = None
        for cond in (
            [s > 0] if ds < 0 else [s < ns - 1] if ds > 0 else []
        ) + ([r > 0] if dr < 0 else [r < nx - 1] if dr > 0 else []):
            ok = cond if ok is None else jnp.logical_and(ok, cond)
        return ok

    def edge(n, ds, dr):
        if dr == 0:
            src, dst = ublk, uside.at[1 if ds < 0 else 0]
        elif dr < 0:
            src, dst = ublk.at[:, pl.ds(0, 2), :], halo.at[1 - ds, :, pl.ds(0, 2), :]
        else:
            src, dst = ublk.at[:, pl.ds(6, 2), :], halo.at[1 - ds, :, pl.ds(6, 2), :]
        return remote(src, dst, sem_cs.at[n], sem_c.at[n], s + ds, r + dr)

    offsets = [(ds, dr) for ds in (-1, 1) for dr in (-1, 1, 0)] + [(0, -1), (0, 1)]
    for n, (ds, dr) in enumerate(offsets):

        @pl.when(exists(ds, dr))
        def _():
            edge(n, ds, dr).start()

        pending.append(
            lambda n=n, ds=ds, dr=dr: pl.when(exists(ds, dr))(lambda: edge(n, ds, dr).wait_send())
        )

    heard(2)
    tell(3)
    for n, (ds, dr) in enumerate(offsets):

        @pl.when(exists(-ds, -dr))
        def _():
            edge(n, ds, dr).wait_recv()

    heard(3)
    def padded(main, rim):
        return jnp.concatenate([main, rim], axis=1)

    field = jnp.concatenate(
        [padded(uside[0], halo[0]), padded(ublk[...], halo[1]), padded(uside[1], halo[2])], axis=0
    )
    slope = tv_slope(field)

    def reduce_all(n, parts):
        red_s[n] = parts
        others = everyone_else(ns, nx, s, r)
        for j, (ds, dr) in enumerate(others):
            remote(red_s.at[n], red_in.at[n, j], sem_s.at[5 + n], sem_r.at[n], ds, dr).start()
        sent(red_in.at[n], sem_s.at[5 + n])
        remote(red_in.at[n], red_in.at[n], sem_s.at[5 + n], sem_r.at[n], s, r).wait_recv()
        even = len(others) // 8 * 8
        sums = jnp.sum(red_in[n, 0:even].reshape(8, even // 8, 1, 128), axis=1)
        return parts + jnp.sum(sums, axis=0) + jnp.sum(red_in[n, even:], axis=0)

    def half(x):
        return x + pltpu.roll(x, 64, 1)

    own_slope = slope[1:3, 0:8, :]
    left = iota((1, 128), 1) < 64
    both = reduce_all(
        0, jnp.where(left, half(lane_partial(gap * gap)), half(lane_partial(own_slope * own_slope)))
    )
    rate = TV_RATE * jnp.sqrt(jnp.sum(jnp.where(left, both, 0.0), axis=1, keepdims=True))
    scale = jnp.sqrt(jnp.sum(jnp.where(left, 0.0, both), axis=1, keepdims=True) + 1e-06)
    inner = field[1:5]
    plane = iota(inner.shape, 0) + jnp.where(s > 0, 1, 0)
    row = iota(inner.shape, 1)
    inside = jnp.logical_and(plane >= 1, iota(inner.shape, 0) < jnp.where(s < ns - 1, 4, 3))
    inside = jnp.logical_and(inside, row < jnp.where(r > 0, 16, 12))
    inside = jnp.logical_and(inside, jnp.logical_or(row < 8, jnp.logical_or(row >= 12, r < nx - 1)))
    step = (rate / scale).reshape(1, 1, 1)
    first_u = jnp.where(inside, inner - step * slope, 0.0)
    slope2 = tv_slope(first_u)[:, 0:8, :]
    both2 = reduce_all(1, lane_partial(slope2 * slope2))
    scale2 = jnp.sqrt(jnp.sum(both2, axis=1, keepdims=True) + 1e-06)
    step2 = (rate / scale2).reshape(1, 1, 1)
    upd_ref[...] = first_u[1:3, 0:8, :] - step2 * slope2

    for wait in pending:
        wait()


def put_out(upd, cor, upd_hbm, cor_hbm, sem):
    copies = [pltpu.make_async_copy(upd, upd_hbm, sem.at[0]), pltpu.make_async_copy(cor, cor_hbm, sem.at[1])]
    for c in copies:
        c.start()
    for c in copies:
        c.wait()


def body(ns, nx, volume, footprint, tile_block, tile_cells, measured):
    any_space = pl.BlockSpec(memory_space=pltpu.HBM)
    vmem = pl.BlockSpec(memory_space=pltpu.VMEM)
    dma = pltpu.SemaphoreType.DMA
    call = pl.pallas_call(
        functools.partial(kernel, ns, nx),
        out_shape=(pltpu.VMEM((2, 8, 512), F32), pltpu.VMEM((2, 1024), F32)),
        in_specs=[any_space] * 5,
        out_specs=(vmem, vmem),
        scratch_shapes=[
            pltpu.VMEM((2, 8, 512), F32),
            pltpu.VMEM((16, 1024, 256), BF16),
            pltpu.VMEM((2, 4, 2, 8), jnp.int32),
            pltpu.VMEM((2, 4, 2, 8), jnp.int32),
            pltpu.VMEM((2, 1024), F32),
            pltpu.VMEM((2, 8, 128), jnp.int32),
            pltpu.VMEM((2, 8, 128), jnp.int32),
            pltpu.VMEM((128, 128), BF16),
            pltpu.VMEM((128, 256), BF16),
            pltpu.VMEM((256, 512), BF16),
            pltpu.VMEM((16, 8, 512), F32),
            pltpu.VMEM((16, 8, 512), F32),
            pltpu.VMEM((2 * nx - 1, 8, 512), F32),
            pltpu.VMEM((8, 512), F32),
            pltpu.VMEM((8, 256), BF16),
            pltpu.VMEM((16, 8, 256), BF16),
            pltpu.VMEM((16, 16, 256), BF16),
            pltpu.VMEM((128, 128), jnp.int32),
            pltpu.VMEM((2, 8, 512), F32),
            pltpu.VMEM((2, 2, 8, 512), F32),
            pltpu.VMEM((3, 2, 8, 512), F32),
            pltpu.VMEM((2, 1, 128), F32),
            pltpu.VMEM((2, ns * nx - 1, 1, 128), F32),
            dma((len(PIECES),)),
            dma((5,)),
            dma((8,)),
            dma((3,)),
            dma((4,)),
            dma((8,)),
            dma((8,)),
            dma((2,)),
            pltpu.SemaphoreType.REGULAR((8,)),
        ],
        compiler_params=pltpu.CompilerParams(
            collective_id=0, has_side_effects=True, vmem_limit_bytes=60 * 1024 * 1024
        ),
    )
    operands = (
        volume,
        footprint.reshape(16, 1024, 256),
        jnp.transpose(tile_block, (0, 2, 3, 1)),
        jnp.transpose(tile_cells, (0, 2, 3, 1)),
        measured,
    )
    results = call(*[pltpu.with_memory_space_constraint(x, pltpu.HBM) for x in operands])
    return pl.pallas_call(
        put_out,
        out_shape=tuple(jax.ShapeDtypeStruct(x.shape, F32) for x in results),
        in_specs=[vmem, vmem],
        out_specs=(any_space, any_space),
        scratch_shapes=[dma((2,))],
        compiler_params=pltpu.CompilerParams(vmem_limit_bytes=1024 * 1024),
    )(*[pltpu.with_memory_space_constraint(x, pltpu.VMEM) for x in results])


def solution(mesh):
    ns, nx = mesh.shape["slab"], mesh.shape["xy"]
    placed = (
        P("slab", "xy", None),
        P("slab", "xy", None, None, None, None),
        P("slab", "xy", None, None),
        P("slab", "xy", None, None),
        P(),
    )
    return jax.shard_map(
        functools.partial(body, ns, nx),
        mesh=mesh,
        in_specs=placed,
        out_specs=(P("slab", "xy", None), P(None, ("slab", "xy"))),
        check_vma=False,
    )
```

```python
import functools

import jax
import jax.numpy as jnp
from jax import lax
from jax.experimental import pallas as pl
from jax.experimental.pallas import tpu as pltpu
from jax.sharding import PartitionSpec as P

TV_RATE = 0.8
SMOOTHING = 0.01
MESH = pl.DeviceIdType.MESH
F32 = jnp.float32
BF16 = jnp.bfloat16
PIECES = ((0, 4), (4, 8), (8, 12), (12, 16))
GROUPS = 12


def iota(shape, dim):
    return lax.broadcasted_iota(jnp.int32, shape, dim)


def lane_next(x):
    return jnp.where(iota(x.shape, 2) < x.shape[2] - 1, pltpu.roll(x, x.shape[2] - 1, 2), 0.0)


def units(field):
    base = field[:-1]
    diff_a = field[1:] - base
    diff_b = pltpu.roll(base, base.shape[1] - 1, 1) - base
    diff_e = lane_next(base) - base
    inv = lax.rsqrt(diff_a * diff_a + diff_b * diff_b + diff_e * diff_e + SMOOTHING)
    return diff_a * inv, diff_b * inv, diff_e * inv


def tv_slope(field):
    unit_a, unit_b, unit_e = units(field)
    core = field[1:-1]
    prev_b = pltpu.roll(unit_b[1:], 1, 1)
    edge = core * lax.rsqrt(core * core + SMOOTHING)
    prev_e = jnp.where(iota(core.shape, 2) == 0, edge, pltpu.roll(unit_e[1:], 1, 2))
    return unit_a[:-1] + prev_b + prev_e - (unit_a + unit_b + unit_e)[1:]


def lane_partial(x):
    rows = jnp.sum(x, axis=0)
    parts = rows[:, :128]
    for c in range(1, x.shape[2] // 128):
        parts = parts + rows[:, c * 128 : (c + 1) * 128]
    return jnp.sum(parts, axis=0, keepdims=True)


def everyone_else(ns, nx, s, r):
    if (ns, nx) != (16, 8):
        return [(lax.rem(s + d // nx, ns), lax.rem(r + d % nx, nx)) for d in range(1, ns * nx)]
    z = ((s // 2) % 2) * 2 + r // 4
    at_x = [((s // 4 + d) % 4) * 4 for d in range(4)]
    at_z = [(z + d) % 4 for d in range(4)]
    at_y = [(r + d) % 4 for d in range(4)]
    at_core = [(s + d) % 2 for d in range(2)]
    slab_z = [(v // 2) * 2 for v in at_z]
    xy_z = [(v % 2) * 4 for v in at_z]
    slab = {
        (dx, dz, dc): at_x[dx] + slab_z[dz] + at_core[dc] for dx in range(4) for dz in range(4) for dc in range(2)
    }
    xy = {(dz, dy): xy_z[dz] + at_y[dy] for dz in range(4) for dy in range(4)}
    moves = [(dx, dz, dy, dc) for dx in range(4) for dz in range(4) for dy in range(4) for dc in range(2)]
    moves.sort(key=lambda m: -sum(min(d, 4 - d) for d in m[:3]) * 2 - m[3])
    return [(slab[dx, dz, dc], xy[dz, dy]) for dx, dz, dy, dc in moves if (dx, dz, dy, dc) != (0, 0, 0, 0)]


def kernel(
    ns, nx,
    vol_hbm, foot_hbm, blk_hbm, cells_hbm, meas_hbm,
    upd_ref, cor_ref,
    vol, wbuf, blk, cells, meas, bcol, ccol, onehot, onehot_t, contrib,
    send_e, send_a, recv_a, total, send_b, recv_b, lhs_b, den,
    ublk, uside, halo,
    red_s, red_in,
    sem_w, sem_in, sem_s, sem_a, sem_b, sem_c, sem_cs, sem_r, sem_k,
):
    s = lax.axis_index("slab")
    r = lax.axis_index("xy")
    groups = wbuf.shape[0]
    low_edge = jnp.logical_and(r < 2, s > 0)
    high_edge = jnp.logical_and(r >= nx - 2, s < ns - 1)
    pending = []
    first = s % 2
    slow_owner = jnp.logical_or(jnp.logical_and(first == 0, r < 2), jnp.logical_and(first == 1, r >= nx - 2))

    ins = [
        pltpu.make_async_copy(blk_hbm, blk, sem_in.at[0]),
        pltpu.make_async_copy(cells_hbm, cells, sem_in.at[1]),
        pltpu.make_async_copy(vol_hbm.at[first], vol.at[0], sem_in.at[2]),
        pltpu.make_async_copy(vol_hbm.at[1 - first], vol.at[1], sem_in.at[4]),
        pltpu.make_async_copy(
            meas_hbm.at[:, pl.ds(pl.multiple_of((s * nx + r) * 1024, 1024), 1024)], meas, sem_in.at[3]
        ),
    ]
    for c in ins:
        c.start()

    def load(n):
        begin, end = PIECES[n]
        source = lax.rem(begin + first * 8, 16)
        return pltpu.make_async_copy(
            foot_hbm.at[pl.ds(source, end - begin)], wbuf.at[pl.ds(begin, end - begin)], sem_w.at[n]
        )

    for n in range(len(PIECES)):
        load(n).start(priority=n // 2)

    barrier = pltpu.get_barrier_semaphore()

    def hello(ds, dr):
        pl.semaphore_signal(barrier, inc=1, device_id=(ds, dr), device_id_type=MESH)

    recv_b[...] = jnp.zeros(recv_b.shape, BF16)
    uside[...] = jnp.zeros(uside.shape, F32)
    recv_a[0 : nx - 1] = jnp.zeros((nx - 1, 8, 512), F32)
    halo[...] = jnp.zeros(halo.shape, F32)

    @pl.when(s > 0)
    def _():
        for d in range(nx):
            hello(s - 1, d)

    @pl.when(s < ns - 1)
    def _():
        for d in range(nx):
            hello(s + 1, d)

    for d in range(1, nx):
        hello(s, lax.rem(r + d, nx))

    ins[0].wait()
    ins[1].wait()
    for p in range(2):
        for t in range(4):
            bcol[p, 2 * t : 2 * t + 2, 0:8] = blk[p, t]
            ccol[p, 2 * t : 2 * t + 2, 0:8] = cells[p, t]
    lane = iota((8, 128), 1)
    view4 = (iota((8, 128), 0) & 1) * 4
    lowest = (4 * s - 1) * 8
    base = (1 - first) * 32
    hots, near_hots = [], []
    for q in range(2):
        blk_p = bcol[(q + first) % 2]
        cells_p = ccol[(q + first) % 2]
        for x in range(8):
            i = q * 8 + x
            near = jnp.broadcast_to(blk_p[:, x : x + 1], (8, 128)) - lowest
            target = (near >> 2) * 8 + view4 + (near & 3)
            hots.append(jnp.where(lane == target, 1.0, 0.0))
            if q == 1:
                near_hots.append(jnp.where(lane == target - base, 1.0, 0.0))
            den[i * 8 : i * 8 + 8, :] = jnp.broadcast_to(cells_p[:, x : x + 1], (8, 128))
    hot = jnp.concatenate(hots, axis=0)
    onehot[0:64, :] = hot[0:64].astype(BF16)
    onehot[64:128, :] = jnp.concatenate(near_hots, axis=0).astype(BF16)
    hot = jnp.transpose(hot)
    for q in range(2):
        part = hot[:, q * 64 : q * 64 + 64]
        onehot_t[:, q * 128 : q * 128 + 128] = jnp.concatenate([part, part], axis=1).astype(BF16)
    ins[2].wait()
    ins[3].wait()
    row16 = iota((16, 128), 0)

    def forward(slot, pair):
        both = []
        for h in range(2):
            i = pair * 2 + h
            vox = vol[slot, pl.ds(i - slot * 8, 1), :]
            parts = []
            for k in range(8):
                t = k // 2
                spread = jnp.broadcast_to(vox[:, t * 128 : (t + 1) * 128], (16, 128))
                parts.append(
                    jnp.where(row16 == k, spread, jnp.where(row16 == k + 8, 1.0, 0.0)).astype(BF16)
                )
            left = jnp.concatenate(parts, axis=1)
            out = jnp.dot(left, wbuf[i], preferred_element_type=F32)
            limit = den[pl.ds(pl.multiple_of(i * 8, 8), 8), :]
            limit = jnp.concatenate([limit, limit], axis=1)
            live = iota((8, 256), 1) < limit
            both.append(
                jnp.concatenate([jnp.where(live, out[0:8], 0.0), jnp.where(live, out[8:16], 0.0)], axis=1)
            )
        whole = jnp.concatenate(both, axis=0)
        high = whole.astype(BF16)
        at = pl.multiple_of(pair * 16 + slot * 64, 16)
        contrib[pl.ds(at, 16), :] = high
        contrib[pl.ds(at + 64, 16), :] = (whole - high.astype(F32)).astype(BF16)

    def forward_slot(slot):
        @pl.loop(slot * 4, slot * 4 + 4)
        def _(pair):
            for n, (begin, _) in enumerate(PIECES):
                if begin // 8 == slot:

                    @pl.when(pair * 2 == begin)
                    def _(n=n):
                        load(n).wait()

            forward(slot, pair)

        k = slice(slot * 128, slot * 128 + 128)
        sums = jnp.dot(onehot_t[:, k], contrib[k, :], preferred_element_type=F32)
        return sums.reshape(16, 8, 512)

    send_e[...] = forward_slot(0)

    pl.semaphore_wait(barrier, nx - 1 + jnp.where(s > 0, nx, 0) + jnp.where(s < ns - 1, nx, 0))

    def remote(src, dst, sem_send, sem_recv, ds, dr):
        return pltpu.make_async_remote_copy(
            src_ref=src, dst_ref=dst, send_sem=sem_send, recv_sem=sem_recv,
            device_id=(ds, dr), device_id_type=MESH,
        )

    rounds = (ns - 2).bit_length()

    def steps(k):
        return [(s - (1 << k), s >= 1 << k), (s + (1 << k), s < ns - (1 << k))] if k < rounds else []

    def tell(k):
        for side, (there, ok) in enumerate(steps(k)):

            @pl.when(ok)
            def _():
                pl.semaphore_signal(sem_k.at[2 * k + 1 - side], inc=1, device_id=(there, r), device_id_type=MESH)

    def heard(k):
        for side, (_, ok) in enumerate(steps(k)):

            @pl.when(ok)
            def _():
                pl.semaphore_wait(sem_k.at[2 * k + side], 1)

    @pl.when(jnp.logical_and(first == 0, s > 0))
    def _():
        for g in range(2):
            remote(send_e.at[g], recv_a.at[nx - 1 + r], sem_s.at[1], sem_a.at[1], s - 1, nx - 2 + g).start()

    @pl.when(jnp.logical_and(first == 1, s < ns - 1))
    def _():
        for g in range(2):
            remote(send_e.at[10 + g], recv_a.at[nx - 1 + r], sem_s.at[2], sem_a.at[1], s + 1, g).start()

    send_a[...] = send_e[...] + forward_slot(1)

    @pl.loop(1, nx)
    def _(d):
        rp = lax.rem(r + d, nx)
        for v, ok in ((0, True), (1, jnp.where(rp % 2 == 0, r <= 4, r >= 3))):
            at = pl.ds(4 * v, 4)

            @pl.when(ok)
            def _(v=v, at=at):
                remote(
                    send_a.at[2 + rp, at], recv_a.at[d - 1, at], sem_s.at[7 * v], sem_a.at[2 * v], s, rp
                ).start()

    @pl.when(jnp.logical_and(first == 1, s > 0))
    def _():
        for g in range(2):
            remote(send_a.at[g], recv_a.at[nx - 1 + r], sem_s.at[1], sem_a.at[1], s - 1, nx - 2 + g).start()

    @pl.when(jnp.logical_and(first == 0, s < ns - 1))
    def _():
        for g in range(2):
            remote(send_a.at[10 + g], recv_a.at[nx - 1 + r], sem_s.at[2], sem_a.at[1], s + 1, g).start()

    def sent(ref, sem, cond=None):
        def wait():
            remote(ref, ref, sem, sem_a.at[0], s, r).wait_send()

        pending.append(wait if cond is None else lambda: pl.when(cond)(wait))

    sent(recv_a.at[pl.ds(0, nx - 1), pl.ds(0, 4)], sem_s.at[0])
    middle = jnp.logical_or(r == 3, r == 4)
    self_half = jnp.where(r % 2 == 0, r <= 4, r >= 3)
    sent(recv_a.at[pl.ds(0, nx - 1), pl.ds(0, 4)], sem_s.at[7], middle)
    outer = jnp.logical_not(middle)
    sent(recv_a.at[pl.ds(0, 3), pl.ds(0, 4)], sem_s.at[7], jnp.logical_and(outer, self_half))
    sent(recv_a.at[pl.ds(0, 4), pl.ds(0, 4)], sem_s.at[7], jnp.logical_and(outer, jnp.logical_not(self_half)))
    sent(recv_a.at[pl.ds(0, 2)], sem_s.at[1], s > 0)
    sent(recv_a.at[pl.ds(0, 2)], sem_s.at[2], s < ns - 1)
    tell(0)
    ins[4].wait()
    m = meas[...]
    seen = jnp.concatenate(
        [m[v : v + 1, q * 256 : (q + 1) * 256] for v in range(2) for q in range(4)], axis=0
    )
    own = send_a[2 + r]
    part = recv_a.at[pl.ds(0, nx - 1), pl.ds(0, 4)]
    remote(part, part, sem_s.at[0], sem_a.at[0], s, r).wait_recv()
    for n, ok in ((4, self_half), (5, jnp.logical_not(self_half))):

        @pl.when(ok)
        def _(n=n):
            part = recv_a.at[pl.ds(0, n), pl.ds(0, 4)]
            remote(part, part, sem_s.at[0], sem_a.at[2], s, r).wait_recv()

    total[...] = own + jnp.sum(recv_a[0 : nx - 1], axis=0)

    @pl.when(jnp.logical_or(low_edge, high_edge))
    def _():
        remote(send_a.at[pl.ds(0, nx)], recv_a.at[pl.ds(nx - 1, nx)], sem_s.at[0], sem_a.at[1], s, r).wait_recv()
        total[...] += jnp.sum(recv_a[nx - 1 : 2 * nx - 1], axis=0)

    tot = total[...]
    corr = (seen - tot[:, 0:256]) / jnp.maximum(tot[:, 256:512], 1.0)
    send_b[...] = corr.astype(BF16)
    recv_b[2 + r] = corr.astype(BF16)

    @pl.when(low_edge)
    def _():
        @pl.loop(0, nx)
        def _(rp):
            remote(send_b, recv_b.at[10 + r], sem_s.at[4], sem_b.at[2], s - 1, rp).start()

    @pl.when(high_edge)
    def _():
        @pl.loop(0, nx)
        def _(rp):
            remote(send_b, recv_b.at[r - (nx - 2)], sem_s.at[4], sem_b.at[1], s + 1, rp).start()

    @pl.loop(1, nx)
    def _(d):
        rp = lax.rem(r + d, nx)
        remote(send_b, recv_b.at[2 + r], sem_s.at[3], sem_b.at[jnp.where(slow_owner, 3, 0)], s, rp).start()

    heard(0)
    tell(1)
    sent(recv_b.at[pl.ds(0, nx - 1)], sem_s.at[3])
    sent(recv_b.at[pl.ds(0, nx)], sem_s.at[4], jnp.logical_or(low_edge, high_edge))
    for v in range(2):
        for q in range(4):
            cor_ref[v : v + 1, q * 256 : (q + 1) * 256] = corr[v * 4 + q : v * 4 + q + 1, :]

    limit = den[...]
    limit = jnp.concatenate([limit, limit], axis=1)
    live = iota((128, 256), 1) < limit
    live3 = jnp.where(live, 1.0, 0.0).reshape(16, 8, 256)

    def arrived(sem, cond, n=2):
        @pl.when(cond)
        def _():
            remote(recv_b.at[pl.ds(0, n)], recv_b.at[pl.ds(0, n)], sem_s.at[3], sem, s, r).wait_recv()

    other_owner = jnp.logical_not(slow_owner)
    row8 = iota((8, 128), 0)

    def back(slot, table):
        half = slice(slot * 64, slot * 64 + 64)
        table = table.astype(F32).reshape(table.shape[0] * 8, 256).astype(BF16)
        hot = onehot[half, :]
        found = jnp.dot(hot, table, preferred_element_type=F32)
        found = jnp.where(live[half], found, 0.0).reshape(8, 8, 256)
        lhs_b[slot * 8 : slot * 8 + 8] = jnp.concatenate([found, live3[slot * 8 : slot * 8 + 8]], axis=1).astype(BF16)
        tops, bottoms = [], []
        for x in range(8):
            i = slot * 8 + x
            out = lax.dot_general(
                lhs_b[i], wbuf[i], (((1,), (1,)), ((), ())), preferred_element_type=F32
            )
            for rows, into in ((out[0:8], tops), (out[8:16], bottoms)):
                lanes = []
                for t in range(4):
                    k = 2 * t
                    both = jnp.where(row8 == k, rows[:, k * 128 : k * 128 + 128], 0.0) + jnp.where(
                        row8 == k + 1, rows[:, k * 128 + 128 : k * 128 + 256], 0.0
                    )
                    lanes.append(jnp.sum(both, axis=0, keepdims=True))
                into.append(jnp.concatenate(lanes, axis=1))
        shift = jnp.concatenate(tops, axis=0) / jnp.concatenate(bottoms, axis=0)
        sart = jnp.maximum(vol[slot] + shift, 0.0)
        ublk[(slot + first) % 2] = sart
        return sart - vol[slot]

    arrived(sem_b.at[0], slow_owner, nx - 2)
    arrived(sem_b.at[0], other_owner, nx - 3)
    arrived(sem_b.at[1], jnp.logical_and(first == 1, s > 0))
    arrived(sem_b.at[2], jnp.logical_and(first == 0, s < ns - 1))
    heard(1)
    tell(2)
    pad = jnp.zeros((8, 8, 256), BF16)
    gap1 = back(1, jnp.concatenate([recv_b[pl.ds((1 - first) * 4, 8)], pad], axis=0))
    arrived(sem_b.at[1], jnp.logical_and(first == 0, s > 0))
    arrived(sem_b.at[2], jnp.logical_and(first == 1, s < ns - 1))
    arrived(sem_b.at[3], slow_owner, 1)
    arrived(sem_b.at[3], other_owner)
    gap0 = back(0, recv_b[...])
    gap = jnp.concatenate([gap0[None], gap1[None]], axis=0)


    def exists(ds, dr):
        ok = None
        for cond in (
            [s > 0] if ds < 0 else [s < ns - 1] if ds > 0 else []
        ) + ([r > 0] if dr < 0 else [r < nx - 1] if dr > 0 else []):
            ok = cond if ok is None else jnp.logical_and(ok, cond)
        return ok

    def edge(n, ds, dr):
        if dr == 0:
            src, dst = ublk, uside.at[1 if ds < 0 else 0]
        elif dr < 0:
            src, dst = ublk.at[:, pl.ds(0, 2), :], halo.at[1 - ds, :, pl.ds(0, 2), :]
        else:
            src, dst = ublk.at[:, pl.ds(6, 2), :], halo.at[1 - ds, :, pl.ds(6, 2), :]
        return remote(src, dst, sem_cs.at[n], sem_c.at[n], s + ds, r + dr)

    offsets = [(ds, dr) for ds in (-1, 1) for dr in (-1, 1, 0)] + [(0, -1), (0, 1)]
    for n, (ds, dr) in enumerate(offsets):

        @pl.when(exists(ds, dr))
        def _():
            edge(n, ds, dr).start()

        pending.append(
            lambda n=n, ds=ds, dr=dr: pl.when(exists(ds, dr))(lambda: edge(n, ds, dr).wait_send())
        )

    heard(2)
    tell(3)
    for n, (ds, dr) in enumerate(offsets):

        @pl.when(exists(-ds, -dr))
        def _():
            edge(n, ds, dr).wait_recv()

    heard(3)
    def padded(main, rim):
        return jnp.concatenate([main, rim], axis=1)

    field = jnp.concatenate(
        [padded(uside[0], halo[0]), padded(ublk[...], halo[1]), padded(uside[1], halo[2])], axis=0
    )
    slope = tv_slope(field)

    def reduce_all(n, parts):
        red_s[n] = parts
        others = everyone_else(ns, nx, s, r)
        for j, (ds, dr) in enumerate(others):
            remote(red_s.at[n], red_in.at[n, j], sem_s.at[5 + n], sem_r.at[n], ds, dr).start()
        sent(red_in.at[n], sem_s.at[5 + n])
        remote(red_in.at[n], red_in.at[n], sem_s.at[5 + n], sem_r.at[n], s, r).wait_recv()
        even = len(others) // 8 * 8
        sums = jnp.sum(red_in[n, 0:even].reshape(8, even // 8, 1, 128), axis=1)
        return parts + jnp.sum(sums, axis=0) + jnp.sum(red_in[n, even:], axis=0)

    def half(x):
        return x + pltpu.roll(x, 64, 1)

    own_slope = slope[1:3, 0:8, :]
    left = iota((1, 128), 1) < 64
    both = reduce_all(
        0, jnp.where(left, half(lane_partial(gap * gap)), half(lane_partial(own_slope * own_slope)))
    )
    rate = TV_RATE * jnp.sqrt(jnp.sum(jnp.where(left, both, 0.0), axis=1, keepdims=True))
    scale = jnp.sqrt(jnp.sum(jnp.where(left, 0.0, both), axis=1, keepdims=True) + 1e-06)
    inner = field[1:5]
    plane = iota(inner.shape, 0) + jnp.where(s > 0, 1, 0)
    row = iota(inner.shape, 1)
    inside = jnp.logical_and(plane >= 1, iota(inner.shape, 0) < jnp.where(s < ns - 1, 4, 3))
    inside = jnp.logical_and(inside, row < jnp.where(r > 0, 16, 12))
    inside = jnp.logical_and(inside, jnp.logical_or(row < 8, jnp.logical_or(row >= 12, r < nx - 1)))
    step = (rate / scale).reshape(1, 1, 1)
    first_u = jnp.where(inside, inner - step * slope, 0.0)
    slope2 = tv_slope(first_u)[:, 0:8, :]
    both2 = reduce_all(1, lane_partial(slope2 * slope2))
    scale2 = jnp.sqrt(jnp.sum(both2, axis=1, keepdims=True) + 1e-06)
    step2 = (rate / scale2).reshape(1, 1, 1)
    upd_ref[...] = first_u[1:3, 0:8, :] - step2 * slope2

    for wait in pending:
        wait()


def put_out(upd, cor, upd_hbm, cor_hbm, sem):
    copies = [pltpu.make_async_copy(upd, upd_hbm, sem.at[0]), pltpu.make_async_copy(cor, cor_hbm, sem.at[1])]
    for c in copies:
        c.start()
    for c in copies:
        c.wait()


def body(ns, nx, volume, footprint, tile_block, tile_cells, measured):
    any_space = pl.BlockSpec(memory_space=pltpu.HBM)
    vmem = pl.BlockSpec(memory_space=pltpu.VMEM)
    dma = pltpu.SemaphoreType.DMA
    call = pl.pallas_call(
        functools.partial(kernel, ns, nx),
        out_shape=(pltpu.VMEM((2, 8, 512), F32), pltpu.VMEM((2, 1024), F32)),
        in_specs=[any_space] * 5,
        out_specs=(vmem, vmem),
        scratch_shapes=[
            pltpu.VMEM((2, 8, 512), F32),
            pltpu.VMEM((16, 1024, 256), BF16),
            pltpu.VMEM((2, 4, 2, 8), jnp.int32),
            pltpu.VMEM((2, 4, 2, 8), jnp.int32),
            pltpu.VMEM((2, 1024), F32),
            pltpu.VMEM((2, 8, 128), jnp.int32),
            pltpu.VMEM((2, 8, 128), jnp.int32),
            pltpu.VMEM((128, 128), BF16),
            pltpu.VMEM((128, 256), BF16),
            pltpu.VMEM((256, 512), BF16),
            pltpu.VMEM((16, 8, 512), F32),
            pltpu.VMEM((16, 8, 512), F32),
            pltpu.VMEM((2 * nx - 1, 8, 512), F32),
            pltpu.VMEM((8, 512), F32),
            pltpu.VMEM((8, 256), BF16),
            pltpu.VMEM((16, 8, 256), BF16),
            pltpu.VMEM((16, 16, 256), BF16),
            pltpu.VMEM((128, 128), jnp.int32),
            pltpu.VMEM((2, 8, 512), F32),
            pltpu.VMEM((2, 2, 8, 512), F32),
            pltpu.VMEM((3, 2, 8, 512), F32),
            pltpu.VMEM((2, 1, 128), F32),
            pltpu.VMEM((2, ns * nx - 1, 1, 128), F32),
            dma((len(PIECES),)),
            dma((5,)),
            dma((8,)),
            dma((3,)),
            dma((4,)),
            dma((8,)),
            dma((8,)),
            dma((2,)),
            pltpu.SemaphoreType.REGULAR((8,)),
        ],
        compiler_params=pltpu.CompilerParams(
            collective_id=0, has_side_effects=True, vmem_limit_bytes=60 * 1024 * 1024
        ),
    )
    operands = (
        volume,
        footprint.reshape(16, 1024, 256),
        jnp.transpose(tile_block, (0, 2, 3, 1)),
        jnp.transpose(tile_cells, (0, 2, 3, 1)),
        measured,
    )
    results = call(*[pltpu.with_memory_space_constraint(x, pltpu.HBM) for x in operands])
    return pl.pallas_call(
        put_out,
        out_shape=tuple(jax.ShapeDtypeStruct(x.shape, F32) for x in results),
        in_specs=[vmem, vmem],
        out_specs=(any_space, any_space),
        scratch_shapes=[dma((2,))],
        compiler_params=pltpu.CompilerParams(vmem_limit_bytes=1024 * 1024),
    )(*[pltpu.with_memory_space_constraint(x, pltpu.VMEM) for x in results])


def solution(mesh):
    ns, nx = mesh.shape["slab"], mesh.shape["xy"]
    placed = (
        P("slab", "xy", None),
        P("slab", "xy", None, None, None, None),
        P("slab", "xy", None, None),
        P("slab", "xy", None, None),
        P(),
    )
    return jax.shard_map(
        functools.partial(body, ns, nx),
        mesh=mesh,
        in_specs=placed,
        out_specs=(P("slab", "xy", None), P(None, ("slab", "xy"))),
        check_vma=False,
    )
```
